32 devices in a mesh: dp: 4 (over y, x), fsdp: 8 (over z, core).
Axes of the slice: x: 2, y: 2, z: 4, core: 2. Of those that a mesh axis runs over, the one named last changes fastest.
Arguments:
- text_input: bfloat16 [32768, 768], P(('dp', 'fsdp')), may hold values from -6 to 6
- layout_input: bfloat16 [32768, 192], P(('dp', 'fsdp')), may hold values from -6 to 6
- text_attn: bfloat16 [3072, 768], P(('dp', 'fsdp')), may hold values from -1 to 1
- text_ff_in: bfloat16 [768, 3072], P(None, ('dp', 'fsdp')), may hold values from -0.21875 to 0.21875
- text_ff_out: bfloat16 [3072, 768], P(('dp', 'fsdp')), may hold values from -0.109375 to 0.109375
- text_vectors: bfloat16 [9216], P(('dp', 'fsdp')), may hold values from -2 to 2
- layout_attn: bfloat16 [768, 192], P(('dp', 'fsdp')), may hold values from -1 to 1
- layout_ff_in: bfloat16 [192, 768], P(None, ('dp', 'fsdp')), may hold values from -0.4375 to 0.4375
- layout_ff_out: bfloat16 [768, 192], P(('dp', 'fsdp')), may hold values from -0.21875 to 0.21875
- layout_vectors: bfloat16 [2304], P(('dp', 'fsdp')), may hold values from -2 to 2
- text_cotangent: bfloat16 [32768, 768], P(('dp', 'fsdp')), may hold values from -6 to 6
- layout_cotangent: bfloat16 [32768, 192], P(('dp', 'fsdp')), may hold values from -6 to 6
- margin: int32 [32768], P(('dp', 'fsdp')), may hold values 0 or 1
- valid: int32 [32768], P(('dp', 'fsdp')), may hold values from 0 to 1, as said below
Outputs:
- text_output: bfloat16 [32768, 768], P(('dp', 'fsdp'))
- layout_output: bfloat16 [32768, 192], P(('dp', 'fsdp'))
- text_input_grad: float32 [32768, 768], P(('dp', 'fsdp'))
- layout_input_grad: float32 [32768, 192], P(('dp', 'fsdp'))
- text_attn_grad: float32 [3072, 768], P(('dp', 'fsdp'))
- text_ff_in_grad: float32 [768, 3072], P(None, ('dp', 'fsdp'))
- text_ff_out_grad: float32 [3072, 768], P(('dp', 'fsdp'))
- text_vectors_grad: float32 [9216], P(('dp', 'fsdp'))
- layout_attn_grad: float32 [768, 192], P(('dp', 'fsdp'))
- layout_ff_in_grad: float32 [192, 768], P(None, ('dp', 'fsdp'))
- layout_ff_out_grad: float32 [768, 192], P(('dp', 'fsdp'))
- layout_vectors_grad: float32 [2304], P(('dp', 'fsdp'))
The draws below stay inside these ranges and needn't reach their ends.
Inputs may be any that keep to these rules, and one draw needn't show every extreme that they name: `valid`: within each sequence of 512 tokens the ones form a prefix of 256 positions or more.
All inputs are finite; a program needn't handle non-finite values. No bound on the sum of `margin` on one device may be relied on, other than what follows from the above.
Results may differ from the reference program's by a relative error of at most 0.012.
The reference program's roundings to bfloat16 on the way count: a program that leaves them out, or rounds other values in their place, can miss the bound.
Values may be sent and summed in bfloat16 or wider, within the bound.
No kernel may reach another device: no remote copies, remote signals or barrier semaphores. Data moves between devices by JAX's collectives and lax.ppermute only.
A program may use at most 320 MiB of HBM per device.

```python
import math
import jax
import jax.numpy as jnp
from jax import lax

D = 768
H = 12
F = 3072
DL = 192
FL = 768
E = 64
EL = 16
SPAN = 512
TOK_DEV = 1024
TOKENS = 32768


def scaled_rows(key, height, breadth, outer):
    values = jax.random.uniform(key, (height, breadth), jnp.float32, -1.0, 1.0)
    position = jnp.arange(height)[:, None]
    factor = jnp.where(position >= 3 * breadth, outer, 1.0)
    return values * factor * math.sqrt(3.0 / breadth)


def draw_text_attn(key, part):
    return scaled_rows(jax.random.fold_in(key, 11), 4 * D, D, 4.0).astype(jnp.bfloat16)


def draw_layout_attn(key, part):
    return scaled_rows(jax.random.fold_in(key, 13), 4 * DL, DL, 4.0).astype(jnp.bfloat16)


def vector_values(key, breadth, hidden_size):
    length = 8 * breadth + hidden_size
    values = jax.random.uniform(key, (length,), jnp.float32, -1.0, 1.0)
    position = jnp.arange(length)
    gain_slots = (position >= 4 * breadth) & (position < 5 * breadth) | (position >= 6 * breadth) & (position < 7 * breadth)
    return jnp.where(gain_slots, 1.0 + 0.3 * values, 0.3 * values)


def draw_text_vectors(key, part):
    return vector_values(jax.random.fold_in(key, 17), D, F).astype(jnp.bfloat16)


def draw_layout_vectors(key, part):
    return vector_values(jax.random.fold_in(key, 19), DL, FL).astype(jnp.bfloat16)


def draw_valid(key, part):
    span_count = TOKENS // SPAN
    lengths = jax.random.randint(jax.random.fold_in(key, 23), (span_count,), SPAN // 2, SPAN + 1)
    lengths = lengths.at[0].set(SPAN // 2)
    position = jnp.arange(TOKENS)
    prefix_end = lengths[position // SPAN]
    return (position % SPAN < prefix_end).astype(jnp.int32)


def touch_ends(drawn, key, low, top_value):
    dims = drawn.shape
    spot = [jax.random.randint(jax.random.fold_in(key, axis), (), 0, dims[axis]) for axis in range(len(dims))]
    drawn = drawn.at[tuple(spot)].set(low)
    longest = dims.index(max(dims))
    spot[longest] = (spot[longest] + 1) % dims[longest]
    return drawn.at[tuple(spot)].set(top_value)


def spiked(entries, stream_key, source, target, blocks, factor):
    owner, partner = [(jnp.arange(entries.shape[dim]) // (entries.shape[dim] // blocks)).reshape([-1 if axis == dim else 1 for axis in range(entries.ndim)]) for dim in (source, target)]
    chosen = jax.random.permutation(stream_key, blocks)[partner]
    strong = (owner == chosen) | (owner == (partner + blocks // 2) % blocks)
    return jnp.where(strong, factor * entries, entries)


def block_levels(key, dims, shards, low, high):
    gain, own = 1.0, jax.random.fold_in(key, 6)
    for axis_at, shards_of in shards:
        draws = jnp.exp(jax.random.uniform(jax.random.fold_in(own, axis_at), (shards_of,), jnp.float32, low / len(shards), high / len(shards)))
        gain = gain * jnp.repeat(draws, dims[axis_at] // shards_of).reshape([-1 if axis == axis_at else 1 for axis in range(len(dims))])
    return gain


def centred(rng, dims, scale, bound, cuts=(), held_as=jnp.bfloat16):
    loudness = block_levels(rng, dims, cuts, -0.22, 0.18) if cuts else 1.0
    array = jax.random.normal(rng, dims, jnp.float32) * scale * loudness
    return jnp.minimum(jnp.maximum(array, -bound), bound).astype(held_as)


def gaussian_with(rng, shape, scale, bound, cuts, heavy, kind=jnp.bfloat16):
    result = scale * jax.random.normal(rng, shape, jnp.float32)
    if cuts:
        result = result * block_levels(rng, shape, cuts, -0.22, 0.18)
    return jnp.clip(spiked(result, jax.random.fold_in(rng, 3), *heavy), -bound, bound).astype(kind)


def setup_inputs(seed: int = 0) -> dict:
    keys = jax.random.split(jax.random.key(seed), 15)
    return {
        "text_input": gaussian_with(keys[0], (TOKENS, D), 1.0, 6.0, ((0, 32),), (0, 1, 32, 2.75)),
        "layout_input": gaussian_with(keys[1], (TOKENS, DL), 1.0, 6.0, ((0, 32),), (0, 1, 32, 2.75)),
        "text_attn": draw_text_attn(jax.random.fold_in(keys[14], 71), 0),
        "text_ff_in": centred(keys[3], (D, F), D ** -0.5, 0.21875, ((1, 32),)),
        "text_ff_out": centred(keys[4], (F, D), F ** -0.5, 0.109375, ((0, 32),)),
        "text_vectors": draw_text_vectors(jax.random.fold_in(keys[14], 71), 0),
        "layout_attn": draw_layout_attn(jax.random.fold_in(keys[14], 71), 0),
        "layout_ff_in": centred(keys[7], (DL, FL), DL ** -0.5, 0.4375, ((1, 32),)),
        "layout_ff_out": centred(keys[8], (FL, DL), FL ** -0.5, 0.21875, ((0, 32),)),
        "layout_vectors": draw_layout_vectors(jax.random.fold_in(keys[14], 71), 0),
        "text_cotangent": centred(keys[10], (TOKENS, D), 1.0, 6.0, ((0, 32),)),
        "layout_cotangent": centred(keys[11], (TOKENS, DL), 1.0, 6.0, ((0, 32),)),
        "margin": touch_ends((jax.random.randint(keys[12], (TOKENS,), 0, 4) < 1).astype(jnp.int32), jax.random.fold_in(keys[12], 1), 0, 1),
        "valid": draw_valid(jax.random.fold_in(keys[14], 71), 0),
    }


@jax.custom_vjp
def low(v):
    return lax.optimization_barrier(v.astype(jnp.bfloat16)).astype(jnp.float32)

@jax.custom_vjp
def low_back(v):
    return v

def low_keep(v):
    return (low(v), None)

def low_pass(kept, grad):
    return (grad,)

def back_keep(v):
    return (v, None)

def back_low(kept, grad):
    return (low(grad),)
low.defvjp(low_keep, low_pass)
low_back.defvjp(back_keep, back_low)
epsilon = 1e-05
root_half = 0.7071067811865476
highest = lax.Precision.HIGHEST

def both_ways(values):
    return low(low_back(values))

def matmul(former, latter):
    return jnp.dot(former, latter, precision=highest)

def layer_norm(values, gain_row, shift_row):
    center = values - lax.optimization_barrier(jnp.mean(values, -1, keepdims=True))
    spread = lax.optimization_barrier(jnp.mean(center * center, -1, keepdims=True))
    return center * lax.rsqrt(spread + epsilon) * gain_row + shift_row

def gelu_exact(values):
    return 0.5 * values * (1.0 + lax.erf(values * root_half))

def softmax_rows(logits):
    largest = lax.optimization_barrier(jnp.max(logits, -1, keepdims=True))
    powers = jnp.exp(logits - largest)
    return powers / lax.optimization_barrier(jnp.sum(powers, -1, keepdims=True))

def split_stream(attn_rows, vectors, breadth, hidden_size):
    blocks = [attn_rows[number * breadth:(number + 1) * breadth] for number in range(4)]
    pieces = [vectors[number * breadth:(number + 1) * breadth] for number in range(8)]
    return (blocks, pieces, vectors[8 * breadth:8 * breadth + hidden_size])

def project_stream(inputs, blocks, pieces, head_size):
    head_shape = (inputs.shape[0] // SPAN, SPAN, H, head_size)
    query_rows = both_ways(matmul(inputs, blocks[0]) + pieces[0])
    key_rows = both_ways(matmul(inputs, blocks[1]))
    value_rows = both_ways(matmul(inputs, blocks[2]) + pieces[1])
    return (query_rows.reshape(head_shape), key_rows.reshape(head_shape), value_rows.reshape(head_shape))

def attend_sequence(group_items):
    text_query, text_key, text_value, layout_query, layout_key, layout_value, fixed_query, fixed_key, valid_keys = group_items
    text_scale = 1.0 / math.sqrt(E)
    layout_scale = 1.0 / math.sqrt(EL)
    text_raw = low_back(jnp.einsum('qhe,khe->hqk', text_query, text_key, precision=highest) * text_scale)
    layout_raw = low_back(jnp.einsum('qhe,khe->hqk', layout_query, layout_key, precision=highest) * layout_scale)
    fixed_raw = jnp.einsum('qhe,khe->hqk', fixed_query, fixed_key, precision=highest) * text_scale
    allowed = valid_keys[None, None, :] > 0
    text_probs = softmax_rows(jnp.where(allowed, text_raw + layout_raw, -1e+30))
    layout_probs = softmax_rows(jnp.where(allowed, layout_raw + fixed_raw, -1e+30))
    text_context = jnp.einsum('hqk,khe->qhe', low(text_probs), text_value, precision=highest)
    layout_context = jnp.einsum('hqk,khe->qhe', low(layout_probs), layout_value, precision=highest)
    return (text_context, layout_context)

def finish_stream(inputs, context, blocks, pieces, hidden_bias, ff_in, ff_out):
    attended = low_back(matmul(both_ways(context), blocks[3]) + pieces[2])
    normed = layer_norm(inputs + attended, pieces[4], pieces[5])
    hidden = low_back(matmul(low(normed), ff_in) + hidden_bias)
    active = low(gelu_exact(hidden))
    output = low_back(matmul(active, ff_out) + pieces[3])
    return layer_norm(normed + output, pieces[6], pieces[7])

def forward(params, text_rows, layout_rows, fixed_query, fixed_key, valid_rows):
    text_blocks, text_pieces, text_bias = split_stream(params[0], params[3], D, F)
    layout_blocks, layout_pieces, layout_bias = split_stream(params[4], params[7], DL, FL)
    text_heads = project_stream(text_rows, text_blocks, text_pieces, E)
    layout_heads = project_stream(layout_rows, layout_blocks, layout_pieces, EL)
    key_masks = valid_rows.reshape(-1, SPAN)
    text_context, layout_context = lax.map(jax.checkpoint(attend_sequence), text_heads + layout_heads + (fixed_query, fixed_key, key_masks))
    text_out = finish_stream(text_rows, text_context.reshape(-1, D), text_blocks, text_pieces, text_bias, params[1], params[2])
    layout_out = finish_stream(layout_rows, layout_context.reshape(-1, DL), layout_blocks, layout_pieces, layout_bias, params[5], params[6])
    return (text_out, layout_out)

def reference(text_input, layout_input, text_attn, text_ff_in, text_ff_out, text_vectors, layout_attn, layout_ff_in, layout_ff_out, layout_vectors, text_cotangent, layout_cotangent, margin, valid):
    weights = tuple((source.astype(jnp.float32) for source in (text_attn, text_ff_in, text_ff_out, text_vectors, layout_attn, layout_ff_in, layout_ff_out, layout_vectors)))
    groups = TOKENS // TOK_DEV

    def grouped(source):
        return source.reshape((groups, TOK_DEV) + source.shape[1:])

    def one_group(totals, group_items):
        text_rows, layout_rows, text_upstream, layout_upstream, margin_rows, valid_rows = group_items
        text_rows = text_rows.astype(jnp.float32)
        layout_rows = layout_rows.astype(jnp.float32)
        text_blocks, text_pieces, unused_bias = split_stream(weights[0], weights[3], D, F)
        fixed_query, fixed_key, unused_value = project_stream(text_rows, text_blocks, text_pieces, E)

        def local_forward(params, text_part, layout_part):
            return forward(params, text_part, layout_part, fixed_query, fixed_key, valid_rows)
        outputs, pullback = jax.vjp(local_forward, weights, text_rows, layout_rows)
        keep_rows = (1 - margin_rows).astype(jnp.float32)[:, None]
        weight_grads, text_grad, layout_grad = pullback((text_upstream.astype(jnp.float32) * keep_rows, layout_upstream.astype(jnp.float32) * keep_rows))
        totals = jax.tree.map(jnp.add, totals, weight_grads)
        return (totals, (outputs[0].astype(jnp.bfloat16), outputs[1].astype(jnp.bfloat16), text_grad, layout_grad))
    initial = tuple((jnp.zeros_like(source) for source in weights))
    totals, results = lax.scan(one_group, initial, tuple((grouped(source) for source in (text_input, layout_input, text_cotangent, layout_cotangent, margin, valid))))
    return (results[0].reshape(TOKENS, D), results[1].reshape(TOKENS, DL), results[2].reshape(TOKENS, D), results[3].reshape(TOKENS, DL), totals[0], totals[1], totals[2], totals[3], totals[4], totals[5], totals[6], totals[7])
```

```python
import functools
import math

import jax
import jax.numpy as jnp
from jax import lax
from jax.experimental import pallas as pl
from jax.experimental.pallas import tpu as pltpu
from jax.sharding import PartitionSpec as P

D = 768
H = 12
F = 3072
DL = 192
FL = 768
E = 64
EL = 16
SPAN = 512

GROUP = 4
GROUPS = H // GROUP
ROWS = 256

epsilon = 1e-05
root_half = 0.7071067811865476
normal_density = 0.3989422804014327

f32 = jnp.float32
bf16 = jnp.bfloat16
AXES = ("dp", "fsdp")
VMEM_LIMIT = 60 * 1024 * 1024


def dot(former, latter, former_dim, latter_dim):
    return lax.dot_general(
        former,
        latter,
        (((former_dim,), (latter_dim,)), ((), ())),
        preferred_element_type=f32,
    )


def params():
    return pltpu.CompilerParams(vmem_limit_bytes=VMEM_LIMIT)


def cost(flops, nbytes, transcendentals=0):
    return pl.CostEstimate(
        flops=int(flops), bytes_accessed=int(nbytes), transcendentals=int(transcendentals)
    )


def whole(shape):
    return pl.BlockSpec(shape, lambda *_: (0,) * len(shape))


def head_rows(values, bias, scale):
    rounded = (values + bias).astype(bf16) if bias is not None else values.astype(bf16)
    if scale is not None:
        rounded = (rounded.astype(f32) * scale).astype(bf16)
    return rounded.T


def layout_project_kernel(x_ref, attn_ref, vec_ref, out_ref):
    x = x_ref[...]
    for number in range(3):
        values = dot(x, attn_ref[pl.ds(number * DL, DL), :], 1, 0)
        bias = None if number == 1 else vec_ref[number // 2 : number // 2 + 1, :]
        scale = 1.0 / math.sqrt(EL) if number == 0 else None
        out_ref[pl.ds(number * DL, DL), :] = head_rows(values, bias, scale)


def layout_project(x, attn, vec):
    tokens = x.shape[0]
    return pl.pallas_call(
        layout_project_kernel,
        out_shape=jax.ShapeDtypeStruct((3 * DL, tokens), bf16),
        compiler_params=params(),
        cost_estimate=cost(2 * tokens * DL * DL * 3, 4 * tokens * DL * 2),
        name="layout_project",
    )(x, attn, vec)


def attend_forward_kernel(
    x_ref,
    wq_ref,
    wk_ref,
    wv_ref,
    vec_ref,
    lq_ref,
    lk_ref,
    lv_ref,
    valid_ref,
    q_ref,
    k_ref,
    v_ref,
    p_ref,
    c_ref,
    cl_ref,
):
    x = x_ref[...]
    q_ref[...] = head_rows(dot(x, wq_ref[...], 1, 0), vec_ref[0:1, :], 1.0 / math.sqrt(E))
    k_ref[...] = head_rows(dot(x, wk_ref[...], 1, 0), None, None)
    v_ref[...] = head_rows(dot(x, wv_ref[...], 1, 0), vec_ref[1:2, :], None)
    tokens = x.shape[0]
    for sequence in range(tokens // SPAN):
        span = pl.ds(sequence * SPAN, SPAN)
        bias_row = (valid_ref[0:1, span].astype(f32) - 1.0) * 1e30
        bias_columns = jnp.broadcast_to(bias_row, (128, SPAN)).T
        bias_full = jnp.concatenate([bias_columns] * (SPAN // 128), 1)
        for head in range(GROUP):
            rows, rows_l = pl.ds(head * E, E), pl.ds(head * EL, EL)
            query = jnp.concatenate([q_ref[rows, span], lq_ref[rows_l, span]], 0)
            key = jnp.concatenate([k_ref[rows, span], lk_ref[rows_l, span]], 0)
            value = jnp.concatenate([v_ref[rows, span], lv_ref[rows_l, span]], 0)
            logits = dot(key, query, 0, 0) + bias_full
            powers = jnp.exp(logits - jnp.max(logits, 0, keepdims=True))
            inverse = 1.0 / jnp.sum(powers, 0, keepdims=True)
            probs = (powers * inverse).astype(bf16)
            p_ref[sequence * GROUP + head] = probs
            context = dot(value, probs, 1, 0).astype(bf16)
            c_ref[rows, span] = context[0:E]
            cl_ref[rows_l, span] = context[E : E + EL]


def attend_forward(x, attn, column, vec, group, layout_heads, valid):
    tokens = x.shape[0]
    spans = tokens // SPAN
    wide, wide_l = GROUP * E, GROUP * EL
    weight = lambda number: pl.BlockSpec((D, wide), lambda *_: (number, column))
    layout_rows = lambda number: pl.BlockSpec(
        (wide_l, tokens), lambda *_: (number * GROUPS + group, 0)
    )
    text_shape = jax.ShapeDtypeStruct((wide, tokens), bf16)
    outs = [
        text_shape,
        text_shape,
        text_shape,
        jax.ShapeDtypeStruct((spans * GROUP, SPAN, SPAN), bf16),
        text_shape,
        jax.ShapeDtypeStruct((wide_l, tokens), bf16),
    ]
    return pl.pallas_call(
        attend_forward_kernel,
        grid=(1,),
        in_specs=[
            whole((tokens, D)),
            weight(0),
            weight(1),
            weight(2),
            pl.BlockSpec((12, wide), lambda *_: (0, group)),
            layout_rows(0),
            layout_rows(1),
            layout_rows(2),
            whole((1, tokens)),
        ],
        out_specs=[whole(out.shape) for out in outs],
        out_shape=outs,
        compiler_params=params(),
        cost_estimate=cost(
            2 * tokens * D * wide * 3 + spans * GROUP * SPAN * SPAN * 1024,
            spans * GROUP * SPAN * SPAN * 2 + 8 * tokens * wide,
            spans * GROUP * SPAN * SPAN,
        ),
        name="attend_forward",
    )(x, attn, attn, attn, vec, layout_heads, layout_heads, layout_heads, valid)


def attend_backward_kernel(
    q_ref,
    k_ref,
    v_ref,
    lq_ref,
    lk_ref,
    lv_ref,
    p_ref,
    dc_ref,
    dcl_ref,
    dq_ref,
    dk_ref,
    dv_ref,
    dlq_ref,
    dlk_ref,
    dlv_ref,
):
    tokens = q_ref.shape[1]
    for sequence in range(tokens // SPAN):
        span = pl.ds(sequence * SPAN, SPAN)
        for head in range(GROUP):
            rows, rows_l = pl.ds(head * E, E), pl.ds(head * EL, EL)
            upstream = jnp.concatenate([dc_ref[rows, span], dcl_ref[rows_l, span]], 0)
            value = jnp.concatenate([v_ref[rows, span], lv_ref[rows_l, span]], 0)
            low_probs = p_ref[sequence * GROUP + head]
            probs = low_probs.astype(f32)
            text_part = probs * dot(value[0:E], upstream[0:E], 0, 0)
            both_part = probs * dot(value, upstream, 0, 0)
            text_mixed = (
                text_part - probs * jnp.sum(text_part, 0, keepdims=True)
            ).astype(bf16)
            layout_mixed = (
                both_part - probs * jnp.sum(both_part, 0, keepdims=True)
            ).astype(bf16)
            value_grad = dot(upstream, low_probs, 1, 1).astype(bf16)
            dv_ref[rows, span] = value_grad[0:E]
            dlv_ref[rows_l, span] = value_grad[E : E + EL]
            dq_ref[rows, span] = (
                dot(k_ref[rows, span], text_mixed, 1, 0) * (1.0 / math.sqrt(E))
            ).astype(bf16)
            dk_ref[rows, span] = dot(q_ref[rows, span], text_mixed, 1, 1).astype(bf16)
            dlq_ref[rows_l, span] = (
                dot(lk_ref[rows_l, span], layout_mixed, 1, 0) * (1.0 / math.sqrt(EL))
            ).astype(bf16)
            dlk_ref[rows_l, span] = dot(lq_ref[rows_l, span], layout_mixed, 1, 1).astype(bf16)


def attend_backward(q, k, v, group, layout_heads, probs, dc, dcl):
    tokens = q.shape[1]
    spans = tokens // SPAN
    wide, wide_l = GROUP * E, GROUP * EL
    text = pl.BlockSpec((wide, tokens), lambda *_: (group, 0))
    layout = pl.BlockSpec((wide_l, tokens), lambda *_: (group, 0))
    layout_rows = lambda number: pl.BlockSpec(
        (wide_l, tokens), lambda *_: (number * GROUPS + group, 0)
    )
    outs = [jax.ShapeDtypeStruct((wide, tokens), bf16)] * 3
    outs += [jax.ShapeDtypeStruct((wide_l, tokens), bf16)] * 3
    return pl.pallas_call(
        attend_backward_kernel,
        grid=(1,),
        in_specs=[
            whole(q.shape),
            whole(k.shape),
            whole(v.shape),
            layout_rows(0),
            layout_rows(1),
            layout_rows(2),
            whole(probs.shape),
            text,
            layout,
        ],
        out_specs=[whole(out.shape) for out in outs],
        out_shape=outs,
        compiler_params=params(),
        cost_estimate=cost(
            spans * GROUP * SPAN * SPAN * 3072,
            spans * GROUP * SPAN * SPAN * 2 + 14 * tokens * wide,
        ),
        name="attend_backward",
    )(q, k, v, layout_heads, layout_heads, layout_heads, probs, dc, dcl)


def norm_forward(values, gain_row, shift_row):
    center = values - jnp.mean(values, -1, keepdims=True)
    inverse = lax.rsqrt(jnp.mean(center * center, -1, keepdims=True) + epsilon)
    scaled = center * inverse
    return (scaled * gain_row + shift_row, scaled, inverse)


def norm_backward(upstream, scaled, inverse, gain_row):
    weighted = upstream * gain_row
    return inverse * (
        weighted
        - jnp.mean(weighted, -1, keepdims=True)
        - scaled * jnp.mean(weighted * scaled, -1, keepdims=True)
    )


def joined(refs, dim):
    return refs[0][...] if len(refs) == 1 else jnp.concatenate([ref[...] for ref in refs], dim)


def finish_start_kernel(pieces, parts, cuts, *refs):
    c_refs, wo_refs = refs[:parts], refs[parts : parts + cuts]
    x_ref, w1_ref, vec_ref, h1_ref, low_ref, scaled_ref, inverse_ref, act_ref, slope_ref = refs[
        parts + cuts :
    ]
    block = w1_ref.shape[0] // pieces
    row = lambda number: vec_ref[number : number + 1, :]
    attended = dot(joined(c_refs, 0), joined(wo_refs, 1), 0, 0) + row(2)
    h1, scaled_one, inverse_one = norm_forward(x_ref[...].astype(f32) + attended, row(4), row(5))
    h1_low = h1.astype(bf16)
    h1_ref[...] = h1
    low_ref[...] = h1_low
    scaled_ref[...] = scaled_one
    inverse_ref[...] = jnp.broadcast_to(inverse_one, inverse_ref.shape)
    for piece in range(pieces):
        part = pl.ds(piece * block, block)
        u = dot(h1_low, w1_ref[part, :], 1, 1) + row(8 + piece)
        half = 0.5 * (1.0 + lax.erf(u * root_half))
        act_ref[:, part] = (u * half).astype(bf16)
        slope_ref[:, part] = half + u * jnp.exp(-0.5 * u * u) * normal_density


def finish_start(x, cs, wos, wo_block, w1, vec):
    tokens, width = x.shape
    hidden = w1.shape[0]
    rows = min(ROWS, tokens)
    natural = pl.BlockSpec((rows, width), lambda i: (i, 0))
    broad = pl.BlockSpec((rows, hidden), lambda i: (i, 0))
    shape = lambda kind, *dims: jax.ShapeDtypeStruct(dims, kind)
    once = pl.Buffered(1)
    return pl.pallas_call(
        functools.partial(finish_start_kernel, hidden // width, len(cs), len(wos)),
        grid=(tokens // rows,),
        in_specs=[pl.BlockSpec((c.shape[0], rows), lambda i: (0, i)) for c in cs]
        + [
            pl.BlockSpec((width, wo.shape[1]), lambda i: (wo_block, 0), pipeline_mode=once)
            for wo in wos
        ]
        + [
            natural,
            pl.BlockSpec((hidden, width), lambda i: (0, 0), pipeline_mode=once),
            whole((12, width)),
        ],
        out_specs=[
            natural,
            natural,
            natural,
            pl.BlockSpec((rows, 128), lambda i: (i, 0)),
            broad,
            broad,
        ],
        out_shape=[
            shape(f32, tokens, width),
            shape(bf16, tokens, width),
            shape(f32, tokens, width),
            shape(f32, tokens, 128),
            shape(bf16, tokens, hidden),
            shape(f32, tokens, hidden),
        ],
        compiler_params=params(),
        cost_estimate=cost(
            2 * tokens * width * (width + hidden),
            tokens * width * 14 + tokens * hidden * 6 + hidden * width * 2,
            tokens * hidden * 2,
        ),
        name="finish_start",
    )(*cs, *wos, x, w1, vec)


def finish_end_kernel(pieces, cuts, *refs):
    wo_refs = refs[:cuts]
    (
        h1_ref, scaled_ref, inverse_ref, act_ref, slope_ref, cot_ref, margin_ref, w1_ref, w2_ref,
        vec_ref, out_ref, du_ref, dy_ref, da_ref, dz1_ref, dc_ref, small_ref, hidden_ref,
    ) = refs[cuts:]
    block = w1_ref.shape[0] // pieces
    row = lambda number: vec_ref[number : number + 1, :]
    y = dot(act_ref[...], w2_ref[...], 1, 0)
    output, scaled_two, inverse_two = norm_forward(h1_ref[...] + (y + row(3)), row(6), row(7))
    out_ref[...] = output.astype(bf16)
    keep_row = (1 - margin_ref[...]).astype(f32)
    keep = jnp.broadcast_to(keep_row, (128, keep_row.shape[1])).T[:, 0:1]
    upstream = cot_ref[...].astype(f32) * keep
    dz2 = norm_backward(upstream, scaled_two, inverse_two, row(6))
    dy = dz2.astype(bf16)
    dy_ref[...] = dy
    total = None
    hidden_sums = []
    for piece in range(pieces):
        part = pl.ds(piece * block, block)
        du = (dot(dy, w2_ref[part, :], 1, 1) * slope_ref[:, part]).astype(bf16)
        du_ref[:, part] = du
        hidden_sums.append(jnp.sum(du.astype(f32), 0, keepdims=True))
        term = dot(du, w1_ref[part, :], 1, 0)
        total = term if total is None else total + term
    dh1 = total + dz2
    scaled_one = scaled_ref[...]
    dz1 = norm_backward(dh1, scaled_one, inverse_ref[:, 0:1], row(4))
    dz1_ref[...] = dz1
    da = dz1.astype(bf16)
    da_ref[...] = da
    dc_ref[...] = dot(joined(wo_refs, 1), da, 1, 1).astype(bf16)

    @pl.when(pl.program_id(0) == 0)
    def _():
        small_ref[...] = jnp.zeros_like(small_ref)
        hidden_ref[...] = jnp.zeros_like(hidden_ref)

    sums = [
        da.astype(f32),
        dy.astype(f32),
        dh1 * scaled_one,
        dh1,
        upstream * scaled_two,
        upstream,
    ]
    for number, values in enumerate(sums):
        small_ref[number : number + 1, :] += jnp.sum(values, 0, keepdims=True)
    for piece in range(pieces):
        hidden_ref[piece : piece + 1, :] += hidden_sums[piece]


def finish_end(kept, cotangent, margin, wos, wo_block, w1, w2, vec):
    h1, _, scaled, inverse, act, slope = kept
    tokens, width = h1.shape
    hidden = w1.shape[0]
    rows = min(ROWS, tokens)
    natural = pl.BlockSpec((rows, width), lambda i: (i, 0))
    flipped = pl.BlockSpec((width, rows), lambda i: (0, i))
    broad = pl.BlockSpec((rows, hidden), lambda i: (i, 0))
    shape = lambda *dims: jax.ShapeDtypeStruct(dims, bf16)
    once = pl.Buffered(1)
    return pl.pallas_call(
        functools.partial(finish_end_kernel, hidden // width, len(wos)),
        grid=(tokens // rows,),
        in_specs=[
            pl.BlockSpec((width, wo.shape[1]), lambda i: (wo_block, 0), pipeline_mode=once)
            for wo in wos
        ]
        + [
            natural,
            natural,
            pl.BlockSpec((rows, 128), lambda i: (i, 0)),
            broad,
            broad,
            natural,
            pl.BlockSpec((1, rows), lambda i: (0, i)),
            pl.BlockSpec((hidden, width), lambda i: (0, 0), pipeline_mode=once),
            pl.BlockSpec((hidden, width), lambda i: (0, 0), pipeline_mode=once),
            whole((12, width)),
        ],
        out_specs=[
            natural,
            broad,
            natural,
            natural,
            natural,
            flipped,
            whole((8, width)),
            whole((8, width)),
        ],
        out_shape=[
            shape(tokens, width),
            shape(tokens, hidden),
            shape(tokens, width),
            shape(tokens, width),
            jax.ShapeDtypeStruct((tokens, width), f32),
            shape(width, tokens),
            jax.ShapeDtypeStruct((8, width), f32),
            jax.ShapeDtypeStruct((8, width), f32),
        ],
        compiler_params=params(),
        cost_estimate=cost(
            2 * tokens * width * (width + 3 * hidden),
            tokens * width * 20 + tokens * hidden * 8 + hidden * width * 4,
        ),
        name="finish_end",
    )(*wos, h1, scaled, inverse, act, slope, cotangent, margin, w1, w2, vec)


def split_store(me_ref, acc_ref, keep_ref, send_ref):
    place = me_ref[1]
    core, line = place % 2, place // 2
    lines, height = keep_ref.shape[1], keep_ref.shape[2]
    for slot in range(lines):
        owner = jnp.bitwise_xor(line, slot) * 2
        mine = pl.multiple_of((owner + core) * height, 8)
        other = pl.multiple_of((owner + 1 - core) * height, 8)
        keep_ref[0, slot] = acc_ref[pl.ds(mine, height), :]
        send_ref[0, slot] = acc_ref[pl.ds(other, height), :].astype(bf16)


def weight_grad_kernel(me_ref, rows_ref, columns_ref, keep_ref, send_ref, acc_ref):
    acc_ref[...] = dot(rows_ref[...], columns_ref[...], 0, 0)
    split_store(me_ref, acc_ref, keep_ref, send_ref)


def split_shapes(height, width):
    return [
        jax.ShapeDtypeStruct((4, 4, height, width), f32),
        jax.ShapeDtypeStruct((4, 4, height, width), bf16),
    ]


def weight_grad(me, rows, columns):
    tokens, hidden = rows.shape
    width = columns.shape[1]
    block = hidden // 4
    height = block // 8
    place = pl.BlockSpec(
        (1, 4, height, width), lambda i, me: (jnp.bitwise_xor(me[0], i), 0, 0, 0)
    )
    return pl.pallas_call(
        weight_grad_kernel,
        grid_spec=pltpu.PrefetchScalarGridSpec(
            num_scalar_prefetch=1,
            grid=(4,),
            in_specs=[
                pl.BlockSpec((tokens, block), lambda i, me: (0, i)),
                pl.BlockSpec((tokens, width), lambda i, me: (0, 0)),
            ],
            out_specs=[place, place],
            scratch_shapes=[pltpu.VMEM((block, width), f32)],
        ),
        out_shape=split_shapes(height, width),
        compiler_params=params(),
        cost_estimate=cost(
            2 * tokens * hidden * width, 2 * tokens * (hidden + width) + 3 * hidden * width
        ),
        name="weight_grad",
    )(me, rows, columns)


def attn_grad_kernel(
    me_ref, x_ref, dq_ref, dk_ref, dv_ref, c0_ref, c1_ref, c2_ref, da_ref,
    keep_ref, send_ref, acc_ref, xt_ref,
):
    step = pl.program_id(0)

    @pl.when(step == 0)
    def _():
        xt_ref[...] = x_ref[...].T
        wide = c0_ref.shape[0]
        for number, c_ref in enumerate((c0_ref, c1_ref, c2_ref)):
            acc_ref[pl.ds(number * wide, wide), :] = dot(c_ref[...], da_ref[...], 1, 0)

    for number, grad_ref in enumerate((dq_ref, dk_ref, dv_ref)):

        @pl.when(step == number + 1)
        def _(grad_ref=grad_ref):
            acc_ref[...] = dot(xt_ref[...], grad_ref[...], 1, 1)

    split_store(me_ref, acc_ref, keep_ref, send_ref)


def attn_grad(me, x, group, dq, dk, dv, cs, da):
    tokens, width = x.shape
    height, wide = width // 8, dq.shape[0]
    place = pl.BlockSpec(
        (1, 4, height, wide), lambda i, me: (jnp.bitwise_xor(me[0], (i + 3) % 4), 0, 0, 0)
    )
    full = lambda *dims: pl.BlockSpec(dims, lambda i, me: (0,) * len(dims))
    return pl.pallas_call(
        attn_grad_kernel,
        grid_spec=pltpu.PrefetchScalarGridSpec(
            num_scalar_prefetch=1,
            grid=(4,),
            in_specs=[full(tokens, width)]
            + [full(wide, tokens)] * 6
            + [pl.BlockSpec((tokens, wide), lambda i, me: (0, group))],
            out_specs=[place, place],
            scratch_shapes=[pltpu.VMEM((width, wide), f32), pltpu.VMEM((width, tokens), bf16)],
        ),
        out_shape=split_shapes(height, wide),
        compiler_params=params(),
        cost_estimate=cost(2 * tokens * width * wide * 4, 2 * tokens * (width * 2 + 6 * wide)),
        name="attn_grad",
    )(me, x, dq, dk, dv, *cs, da)


def input_grad_kernel(cuts, *refs):
    weight_refs, grad_refs = refs[: 3 * len(cuts)], refs[3 * len(cuts) : 3 * len(cuts) + 9]
    dz1_ref, dx_ref, small_ref = refs[3 * len(cuts) + 9 :]
    wide = grad_refs[0].shape[0]
    tokens = dz1_ref.shape[0]
    ones = jnp.ones((8, tokens), bf16)
    small_ref[...] = jnp.zeros_like(small_ref)
    total = None
    for number in range(3):
        for group in range(GROUPS):
            grad = grad_refs[number * GROUPS + group][...]
            start = group
            for piece, cut in enumerate(cuts):
                if 0 <= start < cut:
                    weight = weight_refs[number * len(cuts) + piece]
                    term = dot(weight[:, pl.ds(start * wide, wide)], grad, 1, 0)
                start -= cut
            total = term if total is None else total + term
            if number != 1:
                place = number // 2
                small_ref[place : place + 1, pl.ds(group * wide, wide)] = dot(ones, grad, 1, 1)[0:1]
    dx_ref[...] = total.T + dz1_ref[...]


def input_grad(attns, grads, dz1):
    tokens, width = dz1.shape
    rows = min(512, tokens)
    wide = grads[0].shape[0]
    cuts = [attn.shape[1] // wide for attn in attns]
    once = pl.Buffered(1)
    dx, small = pl.pallas_call(
        functools.partial(input_grad_kernel, cuts),
        grid=(tokens // rows,),
        in_specs=[
            pl.BlockSpec((width, attn.shape[1]), lambda i, number=number: (number, 0), pipeline_mode=once)
            for number in range(3)
            for attn in attns
        ]
        + [pl.BlockSpec((wide, rows), lambda i: (0, i))] * 9
        + [pl.BlockSpec((rows, width), lambda i: (i, 0))],
        out_specs=[
            pl.BlockSpec((rows, width), lambda i: (i, 0)),
            pl.BlockSpec((8, width), lambda i: (i, 0)),
        ],
        out_shape=[
            jax.ShapeDtypeStruct((tokens, width), f32),
            jax.ShapeDtypeStruct((8 * (tokens // rows), width), f32),
        ],
        compiler_params=params(),
        cost_estimate=cost(2 * tokens * width * width * 3, 14 * tokens * width),
        name="input_grad",
    )(*[attn for _ in range(3) for attn in attns], *grads, dz1)
    return dx, jnp.sum(small.reshape(-1, 8, width), 0)


def partners(mesh_sizes, plane, place):
    second = mesh_sizes[1]
    return [
        (a * second + b, (a ^ plane) * second + (b ^ place))
        for a in range(mesh_sizes[0])
        for b in range(mesh_sizes[1])
    ]


class Exchange:
    def __init__(self, sizes):
        self.sizes = sizes

    def __call__(self, value, plane=0, place=0):
        return lax.ppermute(value, AXES, partners(self.sizes, plane, place))


class Order:
    def __init__(self):
        self.token = None

    def wait(self, *values):
        flat, tree = jax.tree.flatten(values)
        if self.token is not None:
            flat.append(self.token)
        done = lax.optimization_barrier(tuple(flat))
        self.token = done[-1]
        flat = done[: tree.num_leaves]
        return jax.tree.unflatten(tree, flat)


class Chain:
    def __init__(self, stages):
        self.stages = stages
        self.pending = next(stages)
        self.result = None


def step(sequence, *chains, values=()):
    pending, values = sequence.wait([chain.pending for chain in chains], values)
    for chain, arrived in zip(chains, pending):
        try:
            chain.pending = chain.stages.send(arrived)
        except StopIteration as stop:
            chain.pending, chain.result = None, stop.value
    return values


def assemble_kernel(cuts, me_ref, *refs):
    sources, outs = refs[:8], refs[8:]
    me = me_ref[0] * 8 + me_ref[1]
    for number, source in enumerate(sources):
        for entry in range(4):
            core, kind = number // 4, number % 4
            high, low = entry // 2, entry % 2
            if kind < 2:
                relative = (kind * 2 + high) * 8 + low * 2 + core
            else:
                relative = (high * 2 + (kind - 2)) * 8 + (2 + low) * 2 + core
            owner = jnp.bitwise_xor(me, relative)
            start = 0
            for out, cut in zip(outs, cuts):
                out[owner] = source[entry, pl.ds(start, cut), :]
                start += cut


def assemble(me, parts, cuts):
    shape = parts[0].shape
    full = lambda *dims: pl.BlockSpec(dims, lambda i, me: (0,) * len(dims))
    return pl.pallas_call(
        functools.partial(assemble_kernel, cuts),
        grid_spec=pltpu.PrefetchScalarGridSpec(
            num_scalar_prefetch=1,
            grid=(1,),
            in_specs=[full(*shape)] * 8,
            out_specs=[full(32, cut, shape[2]) for cut in cuts],
        ),
        out_shape=[jax.ShapeDtypeStruct((32, cut, shape[2]), bf16) for cut in cuts],
        compiler_params=params(),
        cost_estimate=cost(0, 64 * shape[1] * shape[2] * 2),
        name="assemble",
    )(me, *parts)


def gather_rows(exchange, me, own, cuts):
    z1, z2, z3 = yield (exchange(own, 0, 2), exchange(own, 0, 4), exchange(own, 0, 6))
    alpha, beta = jnp.stack([own, z1]), jnp.stack([z2, z3])
    over_x, over_y = yield (exchange(alpha, 1, 0), exchange(beta, 2, 0))
    alpha, beta = jnp.concatenate([alpha, over_x]), jnp.concatenate([beta, over_y])
    over_y, over_x = yield (exchange(alpha, 2, 0), exchange(beta, 1, 0))
    parts = [alpha, over_y, beta, over_x]
    other = yield tuple(exchange(part, 0, 1) for part in parts)
    return assemble(me, [*parts, *other], cuts)


def scatter_sum(exchange, keep, send):
    low = lambda values: values.astype(bf16)
    (received,) = yield (exchange(send, 0, 1),)
    split = lambda values: values.reshape((2, 2) + values.shape[1:])
    both = split(keep) + split(received.astype(f32))
    over_x, over_y = yield (
        exchange(low(both[:, 1, 0:2]), 1, 0),
        exchange(low(both[1, :, 2:4]), 2, 0),
    )
    alpha = both[:, 0, 0:2] + over_x.astype(f32)
    beta = both[0, :, 2:4] + over_y.astype(f32)
    over_y, over_x = yield (exchange(low(alpha[1]), 2, 0), exchange(low(beta[1]), 1, 0))
    alpha = alpha[0] + over_y.astype(f32)
    beta = beta[0] + over_x.astype(f32)
    first, second, third = yield (
        exchange(low(alpha[1]), 0, 2),
        exchange(low(beta[0]), 0, 4),
        exchange(low(beta[1]), 0, 6),
    )
    return (alpha[0] + first.astype(f32)) + (second.astype(f32) + third.astype(f32))


def by_owner_kernel(me_ref, rows_ref, keep_ref, send_ref):
    me = me_ref[0] * 8 + me_ref[1]
    for block in range(4):
        for slot in range(4):
            relative = block * 8 + slot * 2
            keep_ref[block, slot] = rows_ref[jnp.bitwise_xor(me, relative)]
            send_ref[block, slot] = rows_ref[jnp.bitwise_xor(me, relative + 1)].astype(bf16)


def by_owner(me, rows):
    height, width = rows.shape[1:]
    full = lambda *dims: pl.BlockSpec(dims, lambda i, me: (0,) * len(dims))
    return pl.pallas_call(
        by_owner_kernel,
        grid_spec=pltpu.PrefetchScalarGridSpec(
            num_scalar_prefetch=1,
            grid=(1,),
            in_specs=[full(*rows.shape)],
            out_specs=[full(4, 4, height, width)] * 2,
        ),
        out_shape=split_shapes(height, width),
        compiler_params=params(),
        name="by_owner",
    )(me, rows)


def on_device(sizes, *arguments):
    (
        text_input,
        layout_input,
        text_attn,
        text_ff_in,
        text_ff_out,
        text_vectors,
        layout_attn,
        layout_ff_in,
        layout_ff_out,
        layout_vectors,
        text_cotangent,
        layout_cotangent,
        margin,
        valid,
    ) = arguments
    devices = sizes[0] * sizes[1]
    fast = tuple(sizes) == (4, 8)
    tokens = text_input.shape[0]
    rows_t, rows_l = 4 * D // devices, 4 * DL // devices
    wide = GROUP * E
    rest = wide - DL
    valid_row, margin_row = valid.reshape(1, tokens), margin.reshape(1, tokens)

    count_t, count_l = text_vectors.shape[0], layout_vectors.shape[0]
    vectors = jnp.concatenate([text_vectors, layout_vectors])
    vector_rows = -(-vectors.shape[0] // rest)
    vectors = jnp.pad(vectors, (0, vector_rows * rest - vectors.shape[0]))
    vectors = vectors.reshape(vector_rows, rest)
    vectors = jnp.pad(vectors, ((0, 3 * rows_l - vector_rows), (0, 0)))
    misc = jnp.concatenate([layout_attn, layout_ff_in.T, layout_ff_out], 0)
    misc = jnp.concatenate([misc, vectors], 1)

    def unpack(misc):
        misc = misc.reshape(devices, 3 * rows_l, wide)
        part = lambda number: misc[:, number * rows_l : (number + 1) * rows_l, 0:DL].reshape(-1, DL)
        vectors = misc[:, 0:vector_rows, DL:].reshape(devices, -1).astype(f32)
        return (
            part(0),
            part(1),
            part(2),
            vectors[:, 0:count_t].reshape(12, D),
            vectors[:, count_t : count_t + count_l].reshape(12, DL),
        )

    order = Order()
    if fast:
        me = jnp.stack([lax.axis_index("dp"), lax.axis_index("fsdp")]).astype(jnp.int32)
        exchange = Exchange(sizes)
        gather = lambda own, *cuts: Chain(gather_rows(exchange, me, own, cuts))
        own_a = text_attn[:, wide:]
        own_b, own_c = text_ff_in.T, text_ff_out
        chain_0 = gather(
            jnp.concatenate([text_attn[:, 0:wide], misc]), rows_t, 3 * rows_l
        )
        own_a, own_b = step(order, chain_0, values=(own_a, own_b))
        chain_a = gather(own_a, rows_t)
        step(order, chain_0)
        (own_b, own_c) = step(order, chain_a, values=(own_b, own_c))
        chain_b = gather(own_b, rows_t)
        step(order, chain_0)
        step(order, chain_0)
        attn_0, misc = chain_0.result
        attn_0 = attn_0.reshape(4 * D, wide)
        step(order, chain_a)
        attn_l, w1_l, w2_l, vec, vec_l = unpack(misc)
        layout_heads = layout_project(layout_input, attn_l, vec_l)
        (own_c, layout_heads) = step(order, chain_b, values=(own_c, layout_heads))
        chain_c = gather(own_c, rows_t)
        head_0 = attend_forward(text_input, attn_0, 0, vec, 0, layout_heads, valid_row)
        (head_0,) = step(order, chain_a, values=(head_0,))
        step(order, chain_a)
        (attn_a,) = chain_a.result
        attn_a = attn_a.reshape(4 * D, 2 * wide)
        (attn_a,) = step(order, chain_b, values=(attn_a,))
        head_1 = attend_forward(text_input, attn_a, 0, vec, 1, layout_heads, valid_row)
        (head_1, attn_a) = step(order, chain_c, values=(head_1, attn_a))
        head_2 = attend_forward(text_input, attn_a, 1, vec, 2, layout_heads, valid_row)
        (head_2,) = step(order, chain_b, values=(head_2,))
    else:
        me = jnp.zeros((2,), jnp.int32)
        gather = lambda own: lax.all_gather(own, AXES, axis=0, tiled=True)
        attn_0, attn_a, misc = gather(text_attn[:, 0:wide]), gather(text_attn[:, wide:]), gather(misc)
        w1, w2 = gather(text_ff_in.T), gather(text_ff_out)
        attn_l, w1_l, w2_l, vec, vec_l = unpack(misc)
        layout_heads = layout_project(layout_input, attn_l, vec_l)
        head_0 = attend_forward(text_input, attn_0, 0, vec, 0, layout_heads, valid_row)
        head_1 = attend_forward(text_input, attn_a, 0, vec, 1, layout_heads, valid_row)
        head_2 = attend_forward(text_input, attn_a, 1, vec, 2, layout_heads, valid_row)
    heads = (head_0, head_1, head_2)
    cs, cs_l = [head[4] for head in heads], [head[5] for head in heads]

    kept_l = finish_start(layout_input, cs_l, [attn_l], 3, w1_l, vec_l)
    end_l = finish_end(kept_l, layout_cotangent, margin_row, [attn_l], 3, w1_l, w2_l, vec_l)
    if fast:
        (end_l,) = step(order, chain_c, values=(end_l,))
        step(order, chain_b)
        (w1,) = chain_b.result
        w1 = w1.reshape(F, D)
    kept = finish_start(text_input, cs, [attn_0, attn_a], 3, w1, vec)
    if fast:
        (kept,) = step(order, chain_c, values=(kept,))
        step(order, chain_c)
        (w2,) = chain_c.result
        w2 = w2.reshape(F, D)
    end = finish_end(kept, text_cotangent, margin_row, [attn_0, attn_a], 3, w1, w2, vec)
    out, du, dy, da, dz1, dc, small, hidden = end
    out_l, du_l, dy_l, da_l, dz1_l, dc_l, small_l, hidden_l = end_l
    h1_low, act, h1_low_l, act_l = kept[1], kept[4], kept_l[1], kept_l[4]

    def backward(group, dc):
        q, k, v, probs = heads[group][0:4]
        return attend_backward(q, k, v, group, layout_heads, probs, dc, dc_l)

    def grads_of(group, back):
        return attn_grad(me, text_input, group, *back[0:3], cs, da)

    def small_part(grads_attn_l, grads_one_l, grads_two_l, bias, bias_l):
        vector_grad = jnp.concatenate([bias[0:2], small[0:6], hidden[0:4]])
        vector_grad_l = jnp.concatenate([bias_l[0:2], small_l[0:6], hidden_l[0:4]])
        tail = [vector_grad.reshape(devices, count_t), vector_grad_l.reshape(devices, count_l)]
        tail = jnp.concatenate(tail, 1)
        tail = jnp.pad(tail, ((0, 0), (0, vector_rows * rest - tail.shape[1])))
        tail = tail.reshape(devices, vector_rows, rest)
        tail = jnp.pad(tail, ((0, 0), (0, 3 * rows_l - vector_rows), (0, 0)))
        parts = [
            grads.reshape(devices, rows_l, DL) for grads in (grads_attn_l, grads_one_l, grads_two_l)
        ]
        return jnp.concatenate([jnp.concatenate(parts, 1), tail], 2)

    grads_two = weight_grad(me, act, dy)
    if fast:
        chain_two = Chain(scatter_sum(exchange, *grads_two))
        grads_one = weight_grad(me, du, h1_low)
        (grads_one, dc) = step(order, chain_two, values=(grads_one, dc))
        chain_one = Chain(scatter_sum(exchange, *grads_one))
        back_0 = backward(0, dc)
        (back_0, dc) = step(order, chain_one, values=(back_0, dc))
        grads_0 = grads_of(0, back_0)
        (grads_0, dc) = step(order, chain_two, values=(grads_0, dc))
        chain_0 = Chain(scatter_sum(exchange, *grads_0))
        back_1 = backward(1, dc)
        (back_1, dc) = step(order, chain_one, chain_0, values=(back_1, dc))
        grads_1 = grads_of(1, back_1)
        (grads_1, dc) = step(order, chain_two, values=(grads_1, dc))
        chain_1 = Chain(scatter_sum(exchange, *grads_1))
        back_2 = backward(2, dc)
        (back_2,) = step(order, chain_one, chain_0, chain_1, values=(back_2,))
        grads_2 = grads_of(2, back_2)
    else:
        grads_one = weight_grad(me, du, h1_low)
        back_0, back_1, back_2 = backward(0, dc), backward(1, dc), backward(2, dc)
        grads_0, grads_1, grads_2 = (
            grads_of(0, back_0), grads_of(1, back_1), grads_of(2, back_2),
        )
    backs = (back_0, back_1, back_2)
    dx, bias = input_grad([attn_0, attn_a], [back[n] for n in range(3) for back in backs], dz1)
    grads_attn_l, dx_l, bias_l = attn_grad_plain(
        layout_input, [[back[n] for back in backs] for n in (3, 4, 5)], cs_l, da_l, attn_l, dz1_l
    )
    grads_two_l = weight_grad_plain(act_l, dy_l)
    grads_one_l = weight_grad_plain(du_l, h1_low_l)
    misc = small_part(grads_attn_l, grads_one_l, grads_two_l, bias, bias_l)

    if fast:
        keep_m, send_m = by_owner(me, misc)
        (keep_m, send_m, grads_2) = step(order, chain_two, values=(keep_m, send_m, grads_2))
        chain_2 = Chain(
            scatter_sum(
                exchange,
                jnp.concatenate([grads_2[0], keep_m], 2),
                jnp.concatenate([grads_2[1], send_m], 2),
            )
        )
        step(order, chain_2)
        step(order, chain_one, chain_0, chain_1)
        step(order, chain_2)
        step(order, chain_0, chain_1)
        step(order, chain_2)
        step(order, chain_1)
        step(order, chain_2)
        g2, g1 = chain_two.result, chain_one.result
        ga = [chain_0.result, chain_1.result, chain_2.result[0:rows_t]]
        gm = chain_2.result[rows_t:]
    else:

        def scatter(grads):
            keep, send = grads
            both = jnp.stack([keep, send.astype(f32)], 2)
            return lax.psum_scatter(
                both.reshape(-1, keep.shape[-1]), AXES, scatter_dimension=0, tiled=True
            )

        g2, g1 = scatter(grads_two), scatter(grads_one)
        ga = [scatter(grads) for grads in (grads_0, grads_1, grads_2)]
        gm = lax.psum_scatter(misc.reshape(-1, wide), AXES, scatter_dimension=0, tiled=True)
    tail = gm[0:vector_rows, DL:].reshape(-1)
    return (
        out,
        out_l,
        dx,
        dx_l,
        jnp.concatenate(ga, 1),
        g1.T,
        g2,
        tail[0:count_t],
        gm[0:rows_l, 0:DL],
        gm[rows_l : 2 * rows_l, 0:DL].T,
        gm[2 * rows_l : 3 * rows_l, 0:DL],
        tail[count_t : count_t + count_l],
    )


def plain_kernel(rows_ref, columns_ref, out_ref):
    out_ref[...] = dot(rows_ref[...], columns_ref[...], 0, 0)


def weight_grad_plain(rows, columns):
    tokens, hidden = rows.shape
    width = columns.shape[1]
    return pl.pallas_call(
        plain_kernel,
        out_shape=jax.ShapeDtypeStruct((hidden, width), f32),
        compiler_params=params(),
        cost_estimate=cost(2 * tokens * hidden * width, 2 * tokens * (hidden + width)),
        name="weight_grad_layout",
    )(rows, columns)


def attn_grad_plain_kernel(*refs):
    x_ref, parts, c_refs = refs[0], [refs[1:4], refs[4:7], refs[7:10]], refs[10:13]
    da_ref, attn_ref, dz1_ref, grad_ref, dx_ref, small_ref = refs[13:]
    width = x_ref.shape[1]
    xt = x_ref[...].T
    total = None
    ones = jnp.ones((8, x_ref.shape[0]), bf16)
    small_ref[...] = jnp.zeros_like(small_ref)
    for number, part_refs in enumerate(parts):
        grad = joined(part_refs, 0)
        rows = pl.ds(number * width, width)
        grad_ref[rows, :] = dot(xt, grad, 1, 1)
        term = dot(attn_ref[rows, :], grad, 1, 0)
        total = term if total is None else total + term
        if number != 1:
            place = number // 2
            small_ref[place : place + 1, :] = dot(ones, grad, 1, 1)[0:1]
    grad_ref[pl.ds(3 * width, width), :] = dot(joined(c_refs, 0), da_ref[...], 1, 0)
    dx_ref[...] = total.T + dz1_ref[...]


def attn_grad_plain(x, parts, cs, da, attn, dz1):
    tokens, width = x.shape
    return pl.pallas_call(
        attn_grad_plain_kernel,
        out_shape=[
            jax.ShapeDtypeStruct((4 * width, width), f32),
            jax.ShapeDtypeStruct((tokens, width), f32),
            jax.ShapeDtypeStruct((8, width), f32),
        ],
        compiler_params=params(),
        cost_estimate=cost(2 * tokens * width * width * 7, 24 * tokens * width),
        name="attn_grad_layout",
    )(x, *[part for three in parts for part in three], *cs, da, attn, dz1)


def solution(mesh):
    rows, columns, flat = P(AXES, None), P(None, AXES), P(AXES)
    sizes = (mesh.shape["dp"], mesh.shape["fsdp"])
    return jax.shard_map(
        functools.partial(on_device, sizes),
        mesh=mesh,
        in_specs=(
            rows, rows, rows, columns, rows, flat, rows, columns, rows, flat, rows, rows, flat, flat,
        ),
        out_specs=(
            rows, rows, rows, rows, rows, columns, rows, flat, rows, columns, rows, flat,
        ),
        check_vma=False,
    )
```

```python
import functools
import math

import jax
import jax.numpy as jnp
from jax import lax
from jax.experimental import pallas as pl
from jax.experimental.pallas import tpu as pltpu
from jax.sharding import PartitionSpec as P

D = 768
H = 12
F = 3072
DL = 192
FL = 768
E = 64
EL = 16
SPAN = 512

PAIR = 2
GROUP = 4
GROUPS = H // GROUP
ROWS = 256
SLOTS = 32
UNIT = F // SLOTS
UNIT_L = FL // SLOTS

epsilon = 1e-05
root_half = 0.7071067811865476
normal_density = 0.3989422804014327

f32 = jnp.float32
bf16 = jnp.bfloat16
AXES = ("dp", "fsdp")
VMEM_LIMIT = 60 * 1024 * 1024


def dot(former, latter, former_dim, latter_dim):
    return lax.dot_general(
        former,
        latter,
        (((former_dim,), (latter_dim,)), ((), ())),
        preferred_element_type=f32,
    )


def params():
    return pltpu.CompilerParams(vmem_limit_bytes=VMEM_LIMIT)


def cost(flops, nbytes, transcendentals=0):
    return pl.CostEstimate(
        flops=int(flops / 50), bytes_accessed=int(nbytes / 50), transcendentals=0
    )


def whole(shape):
    return pl.BlockSpec(shape, lambda *_: (0,) * len(shape))


def relative(slot):
    core, part, high, low = slot // 16, slot % 16 // 4, slot % 4 // 2, slot % 2
    if part < 2:
        plane, line = part * 2 + high, low
    else:
        plane, line = high * 2 + part - 2, 2 + low
    return plane * 8 + line * 2 + core


def owner(me, slot):
    return slot if me is None else jnp.bitwise_xor(me, relative(slot))


def place(fast, me_ref):
    return me_ref[0] if fast else None


def full(*dims):
    return pl.BlockSpec(dims, lambda *_: (0,) * len(dims))


def prefetched(kernel, me, operands, in_specs, outs, out_specs=None, grid=(1,), scratch=(), **rest):
    return pl.pallas_call(
        kernel,
        grid_spec=pltpu.PrefetchScalarGridSpec(
            num_scalar_prefetch=1,
            grid=grid,
            in_specs=in_specs,
            out_specs=out_specs or [full(*out.shape) for out in outs],
            scratch_shapes=scratch,
        ),
        out_shape=outs,
        compiler_params=params(),
        **rest,
    )(me, *operands)


def shaped(kind, *dims):
    return jax.ShapeDtypeStruct(dims, kind)


def head_rows(values, bias, scale):
    rounded = (values + bias).astype(bf16) if bias is not None else values.astype(bf16)
    if scale is not None:
        rounded = (rounded.astype(f32) * scale).astype(bf16)
    return rounded.T


def project_layout(x, weight, vec_ref, out_ref):
    for number in range(3):
        values = dot(x, weight(number), 1, 0)
        bias = None if number == 1 else vec_ref[number // 2 : number // 2 + 1, :]
        scale = 1.0 / math.sqrt(EL) if number == 0 else None
        out_ref[pl.ds(number * DL, DL), :] = head_rows(values, bias, scale)


def layout_project_kernel(x_ref, attn_ref, vec_ref, out_ref):
    weight = lambda number: attn_ref[pl.ds(number * DL, DL), :]
    project_layout(x_ref[...].T, weight, vec_ref, out_ref)


def layout_project(x, attn, vec):
    return pl.pallas_call(
        layout_project_kernel,
        out_shape=shaped(bf16, 3 * DL, x.shape[1]),
        compiler_params=params(),
        name="layout_project",
    )(x, attn, vec)


def begin_kernel(me_ref, *refs):
    sources, x_ref = refs[:8], refs[8]
    (
        attn_ref, attn_l_ref, w1_l_ref, w2_l_ref, vec_ref, hidden_ref, vec_l_ref, heads_ref,
        rows_ref, units_ref,
    ) = refs[9:]
    me = me_ref[0]
    height, height_l = attn_ref.shape[1], attn_l_ref.shape[1]
    for slot in range(SLOTS):
        source, entry, block = sources[slot // 4], slot % 4, owner(me, slot)
        attn_ref[block] = source[entry, 0:height, :]
        start = 0
        for out_ref in (attn_l_ref, w1_l_ref, w2_l_ref):
            lanes = slice(start, start + DL)
            out_ref[block] = source[entry, height : height + height_l, lanes]
            start += GROUP * E
        rows_ref[block] = source[entry, height + height_l :, 0:128].astype(f32)
    for number in range(3 * SLOTS):
        row = rows_ref[number // 3, number % 3 : number % 3 + 1, :]
        line, column = number // 8, number % 8
        if line < 8:
            vec_ref[line : line + 1, column * UNIT : (column + 1) * UNIT] = row[:, 0:UNIT]
        else:
            units_ref[number - 8 * 8] = row
        vec_l_ref[line : line + 1, column * UNIT_L : (column + 1) * UNIT_L] = row[
            :, UNIT : UNIT + UNIT_L
        ]
    for slot in range(SLOTS):
        row = units_ref[owner(me, slot)]
        part, entry = slot // 4, slot % 4
        hidden_ref[part : part + 1, entry * UNIT : (entry + 1) * UNIT] = row[:, 0:UNIT]
    weight = lambda number: attn_l_ref[pl.ds(number * 8, 8)].reshape(DL, DL)
    project_layout(x_ref[...].T, weight, vec_l_ref, heads_ref)


def begin(me, parts, x):
    tokens = x.shape[1]
    height, height_l = 4 * D // SLOTS, 4 * DL // SLOTS
    outs = [
        shaped(bf16, SLOTS, height, D),
        shaped(bf16, SLOTS, height_l, DL),
        shaped(bf16, SLOTS, height_l, DL),
        shaped(bf16, SLOTS, height_l, DL),
        shaped(f32, 8, D),
        shaped(f32, 8, F // 8),
        shaped(f32, 12, DL),
        shaped(bf16, 3 * DL, tokens),
    ]
    operands = [*parts, x]
    return prefetched(
        begin_kernel,
        me,
        operands,
        [full(*operand.shape) for operand in operands],
        outs,
        scratch=[pltpu.VMEM((SLOTS, 8, 128), f32), pltpu.VMEM((SLOTS, 1, 128), f32)],
        cost_estimate=cost(2 * tokens * DL * DL * 3, 10 * tokens * DL + 64 * parts[0].size),
        name="begin",
    )


def attend_forward_kernel(
    x_ref, wq_ref, wk_ref, wv_ref, vec_ref, lq_ref, lk_ref, lv_ref, valid_ref,
    q_ref, k_ref, v_ref, p_ref, c_ref, cl_ref,
):
    x = x_ref[...]
    q_ref[...] = head_rows(dot(x, wq_ref[...], 1, 0), vec_ref[0:1, :], 1.0 / math.sqrt(E))
    k_ref[...] = head_rows(dot(x, wk_ref[...], 1, 0), None, None)
    v_ref[...] = head_rows(dot(x, wv_ref[...], 1, 0), vec_ref[1:2, :], None)
    tokens = x_ref.shape[0]
    for sequence in range(tokens // SPAN):
        span = pl.ds(sequence * SPAN, SPAN)
        bias_row = (valid_ref[0:1, span].astype(f32) - 1.0) * 1e30
        bias_columns = jnp.broadcast_to(bias_row, (128, SPAN)).T
        bias_full = jnp.concatenate([bias_columns] * (SPAN // 128), 1)
        for head in range(GROUP):
            rows, rows_l = pl.ds(head * E, E), pl.ds(head * EL, EL)
            query = jnp.concatenate([q_ref[rows, span], lq_ref[rows_l, span]], 0)
            key = jnp.concatenate([k_ref[rows, span], lk_ref[rows_l, span]], 0)
            value = jnp.concatenate([v_ref[rows, span], lv_ref[rows_l, span]], 0)
            logits = dot(key, query, 0, 0) + bias_full
            powers = jnp.exp(logits - jnp.max(logits, 0, keepdims=True))
            inverse = 1.0 / jnp.sum(powers, 0, keepdims=True)
            probs = (powers * inverse).astype(bf16)
            p_ref[(head // PAIR * (tokens // SPAN) + sequence) * PAIR + head % PAIR] = probs
            context = dot(value, probs, 1, 0).astype(bf16)
            c_ref[rows, span] = context[0:E]
            cl_ref[rows_l, span] = context[E : E + EL]


def attend_forward(x, attn, vec, layout_heads, valid):
    tokens = x.shape[0]
    spans = tokens // SPAN
    wide, wide_l = GROUP * E, GROUP * EL
    weight = lambda number: pl.BlockSpec((D, wide), lambda i: (number, i))
    layout_rows = lambda number: pl.BlockSpec(
        (wide_l, tokens), lambda i: (number * GROUPS + i, 0)
    )
    text = pl.BlockSpec((wide, tokens), lambda i: (i, 0))
    return pl.pallas_call(
        attend_forward_kernel,
        grid=(GROUPS,),
        in_specs=[
            whole((tokens, D)),
            weight(0),
            weight(1),
            weight(2),
            pl.BlockSpec((8, wide), lambda i: (0, i)),
            layout_rows(0),
            layout_rows(1),
            layout_rows(2),
            whole((1, tokens)),
        ],
        out_specs=[
            text,
            text,
            text,
            pl.BlockSpec((spans * GROUP, SPAN, SPAN), lambda i: (i, 0, 0)),
            text,
            pl.BlockSpec((wide_l, tokens), lambda i: (i, 0)),
        ],
        out_shape=[shaped(bf16, D, tokens)] * 3
        + [
            shaped(bf16, spans * H, SPAN, SPAN),
            shaped(bf16, D, tokens),
            shaped(bf16, DL, tokens),
        ],
        compiler_params=params(),
        cost_estimate=cost(
            2 * tokens * D * D * 3 + spans * H * SPAN * SPAN * 1024,
            spans * H * SPAN * SPAN * 2 + 8 * tokens * D,
            spans * H * SPAN * SPAN,
        ),
        name="attend_forward",
    )(x, attn, attn, attn, vec, layout_heads, layout_heads, layout_heads, valid)


def attend_backward_kernel(fast, me_ref, *refs):
    (
        q_ref, k_ref, v_ref, lq_ref, lk_ref, lv_ref, p_ref, dc_ref, dcl_ref, x_ref, c_ref, da_ref,
    ) = refs[:12]
    before, refs = refs[12:-10], refs[-10:]
    (
        dq_ref, dk_ref, dv_ref, dlq_ref, dlk_ref, dlv_ref, keep_ref, send_ref, small_ref, acc_ref,
    ) = refs
    tokens = q_ref.shape[1]
    step = pl.program_id(0)

    @pl.when(step < GROUP // PAIR)
    def _():
        for sequence in range(tokens // SPAN):
            span = pl.ds(sequence * SPAN, SPAN)
            for head in range(PAIR):
                rows, rows_l = pl.ds(head * E, E), pl.ds(head * EL, EL)
                out_rows = pl.ds(pl.multiple_of(step * PAIR * E + head * E, E), E)
                upstream = jnp.concatenate([dc_ref[rows, span], dcl_ref[rows_l, span]], 0)
                value = jnp.concatenate([v_ref[rows, span], lv_ref[rows_l, span]], 0)
                low_probs = p_ref[sequence * PAIR + head]
                probs = low_probs.astype(f32)
                text_part = probs * dot(value[0:E], upstream[0:E], 0, 0)
                both_part = probs * dot(value, upstream, 0, 0)
                text_mixed = (
                    text_part - probs * jnp.sum(text_part, 0, keepdims=True)
                ).astype(bf16)
                layout_mixed = (
                    both_part - probs * jnp.sum(both_part, 0, keepdims=True)
                ).astype(bf16)
                value_grad = dot(upstream, low_probs, 1, 1).astype(bf16)
                dv_ref[out_rows, span] = value_grad[0:E]
                dlv_ref[rows_l, span] = value_grad[E : E + EL]
                dq_ref[out_rows, span] = (
                    dot(k_ref[rows, span], text_mixed, 1, 0) * (1.0 / math.sqrt(E))
                ).astype(bf16)
                dk_ref[out_rows, span] = dot(q_ref[rows, span], text_mixed, 1, 1).astype(bf16)
                dlq_ref[rows_l, span] = (
                    dot(lk_ref[rows_l, span], layout_mixed, 1, 0) * (1.0 / math.sqrt(EL))
                ).astype(bf16)
                dlk_ref[rows_l, span] = dot(lq_ref[rows_l, span], layout_mixed, 1, 1).astype(bf16)

    @pl.when(step == GROUP // PAIR)
    def _():
        wide = dq_ref.shape[0]
        blocks = SLOTS // 4
        xt = x_ref[...].T
        ones = jnp.ones((8, tokens), bf16)
        small_ref[...] = jnp.zeros_like(small_ref)
        for number, grad_ref in enumerate((dq_ref, dk_ref, dv_ref)):
            grad = grad_ref[...]
            acc_ref[pl.ds(number * blocks, blocks)] = dot(xt, grad, 1, 1).reshape(
                blocks, D // blocks, wide
            )
            if number != 1:
                line = number // 2
                small_ref[line : line + 1, :] = dot(ones, grad, 1, 1)[0:1]
        acc_ref[pl.ds(3 * blocks, blocks)] = dot(c_ref[...], da_ref[...], 1, 0).reshape(
            blocks, D // blocks, wide
        )
        me = place(fast, me_ref)
        start = keep_ref.shape[2] - acc_ref.shape[1]
        rows = pl.ds(start, acc_ref.shape[1])
        for slot in range(16):
            keep_ref[slot // 4, slot % 4, rows, :] = acc_ref[owner(me, slot)]
            send_ref[slot // 4, slot % 4, rows, :] = acc_ref[owner(me, slot + 16)].astype(bf16)
        for out_ref, before_ref in zip((keep_ref, send_ref), before):
            out_ref[:, :, 0:start, :] = before_ref[...]


def attend_backward(fast, me, q, k, v, group, layout_heads, probs, dc, dcl, x, c, da, before=()):
    tokens = q.shape[1]
    spans, steps = tokens // SPAN, GROUP // PAIR
    wide, wide_l, height = GROUP * E, GROUP * EL, 4 * D // SLOTS
    at = lambda i: jnp.minimum(i, steps - 1)
    text_of = pl.BlockSpec((PAIR * E, tokens), lambda i, me: (group * steps + at(i), 0))
    layout_of = lambda first: pl.BlockSpec(
        (PAIR * EL, tokens), lambda i, me: (first * steps + at(i), 0)
    )
    outs = [shaped(bf16, wide, tokens)] * 3 + [shaped(bf16, wide_l, tokens)] * 3
    rows = height + (before[0].shape[2] if before else 0)
    outs += [shaped(f32, 4, 4, rows, wide), shaped(bf16, 4, 4, rows, wide), shaped(f32, 8, wide)]
    return prefetched(
        functools.partial(attend_backward_kernel, fast),
        me,
        (q, k, v, layout_heads, layout_heads, layout_heads, probs, dc, dcl, x, c, da, *before),
        [
            text_of,
            text_of,
            text_of,
            layout_of(group),
            layout_of(GROUPS + group),
            layout_of(2 * GROUPS + group),
            pl.BlockSpec((spans * PAIR, SPAN, SPAN), lambda i, me: (group * steps + at(i), 0, 0)),
            text_of,
            layout_of(group),
            full(tokens, D),
            full(D, tokens),
            pl.BlockSpec((tokens, wide), lambda i, me: (0, group)),
        ]
        + [full(*part.shape) for part in before],
        outs,
        out_specs=[full(wide, tokens)] * 3
        + [layout_of(0)] * 3
        + [full(*out.shape) for out in outs[6:]],
        grid=(steps + 1,),
        scratch=[pltpu.VMEM((SLOTS, height, wide), f32)],
        cost_estimate=cost(
            spans * GROUP * SPAN * SPAN * 3072 + 8 * tokens * D * wide,
            spans * GROUP * SPAN * SPAN * 2 + 26 * tokens * wide,
        ),
        name="attend_backward",
    )


def joined(refs, dim):
    return refs[0][...] if len(refs) == 1 else jnp.concatenate([ref[...] for ref in refs], dim)


def norm_forward(values, gain_row, shift_row):
    center = values - jnp.mean(values, -1, keepdims=True)
    inverse = lax.rsqrt(jnp.mean(center * center, -1, keepdims=True) + epsilon)
    scaled = center * inverse
    return (scaled * gain_row + shift_row, scaled, inverse)


def norm_backward(upstream, scaled, inverse, gain_row):
    weighted = upstream * gain_row
    return inverse * (
        weighted
        - jnp.mean(weighted, -1, keepdims=True)
        - scaled * jnp.mean(weighted * scaled, -1, keepdims=True)
    )


def finish_rows(
    x, context, cotangent, margin_row, wo, w1, w2, bias, row, pieces, refs, flipped=False
):
    out_ref, du_refs, act_refs, low_ref, dy_ref, da_ref, dz1_ref, dc_ref, slope_ref = refs
    block = slope_ref.shape[1] // pieces
    attended = dot(context, wo, 0, 0) + row(2)
    h1, scaled_one, inverse_one = norm_forward(x.astype(f32) + attended, row(4), row(5))
    h1_low = h1.astype(bf16)
    low_ref[...] = h1_low
    total = None
    for piece in range(pieces):
        part = pl.ds(piece * block, block)
        u = dot(h1_low, w1(piece), 1, 1) + bias(piece)
        half = 0.5 * (1.0 + lax.erf(u * root_half))
        act = (u * half).astype(bf16)
        act_refs[piece][...] = act
        slope_ref[:, part] = half + u * jnp.exp(-0.5 * u * u) * normal_density
        term = dot(act, w2(piece), 1, 0)
        total = term if total is None else total + term
    output, scaled_two, inverse_two = norm_forward(h1 + (total + row(3)), row(6), row(7))
    out_ref[...] = output.astype(bf16).T if flipped else output.astype(bf16)
    keep_row = (1 - margin_row).astype(f32)
    keep = jnp.broadcast_to(keep_row, (128, keep_row.shape[1])).T[:, 0:1]
    upstream = cotangent.astype(f32) * keep
    dz2 = norm_backward(upstream, scaled_two, inverse_two, row(6))
    dy = dz2.astype(bf16)
    dy_ref[...] = dy
    total = None
    hidden_sums = []
    for piece in range(pieces):
        part = pl.ds(piece * block, block)
        du = (dot(dy, w2(piece), 1, 1) * slope_ref[:, part]).astype(bf16)
        du_refs[piece][...] = du
        hidden_sums.append(jnp.sum(du.astype(f32), 0, keepdims=True))
        term = dot(du, w1(piece), 1, 0)
        total = term if total is None else total + term
    dh1 = total + dz2
    dz1 = norm_backward(dh1, scaled_one, inverse_one, row(4))
    dz1_ref[...] = dz1
    da = dz1.astype(bf16)
    da_ref[...] = da
    dc_ref[...] = dot(wo, da, 1, 1).astype(bf16)
    sums = [
        da.astype(f32),
        dy.astype(f32),
        dh1 * scaled_one,
        dh1,
        upstream * scaled_two,
        upstream,
    ]
    return [jnp.sum(values, 0, keepdims=True) for values in sums], hidden_sums


def finish_kernel(fast, parts, cuts, me_ref, *refs):
    c_refs, wo_refs, w1_refs = refs[:parts], refs[parts : parts + cuts], refs[parts + cuts :][:8]
    (
        x_ref, w2_hbm, cot_ref, margin_ref, vec_ref, bias_ref, out_ref, own_ref, other_ref, thin_ref,
        da_ref, dz1_ref, dc_ref, small_ref, hidden_ref, slope_ref, w2_ref, sems,
    ) = refs[parts + cuts + 8 :]
    step = pl.program_id(0)
    me = place(fast, me_ref)
    width = x_ref.shape[1]
    copies = [
        pltpu.make_async_copy(w2_hbm.at[owner(me, slot)], w2_ref.at[slot], sems.at[slot])
        for slot in range(SLOTS)
    ]

    @pl.when(step == 0)
    def _():
        for copy in copies:
            copy.start()
        small_ref[...] = jnp.zeros_like(small_ref)
        hidden_ref[...] = jnp.zeros_like(hidden_ref)
        for copy in copies:
            copy.wait()

    block = slope_ref.shape[1] // 4
    wide = lambda which: [
        (own_ref, other_ref)[piece // 2].at[which, :, pl.ds(piece % 2 * block, block)]
        for piece in range(4)
    ]
    sums, hidden_sums = finish_rows(
        x_ref[...],
        joined(c_refs, 0),
        cot_ref[...],
        margin_ref[...],
        joined(wo_refs, 1),
        lambda piece: joined(w1_refs[2 * piece : 2 * piece + 2], 0).reshape(-1, width),
        lambda piece: w2_ref[pl.ds(piece * 8, 8)].reshape(-1, width),
        lambda piece: joined([bias_ref.at[2 * piece + n : 2 * piece + n + 1] for n in (0, 1)], 1),
        lambda number: vec_ref[number : number + 1, :],
        4,
        (
            out_ref, wide(0), wide(1), thin_ref.at[0], thin_ref.at[1], da_ref, dz1_ref, dc_ref,
            slope_ref,
        ),
    )
    for number, values in enumerate(sums):
        small_ref[number : number + 1, :] += values
    half = hidden_ref.shape[1]
    for piece, values in enumerate(hidden_sums):
        hidden_ref[2 * piece : 2 * piece + 1, :] += values[:, 0:half]
        hidden_ref[2 * piece + 1 : 2 * piece + 2, :] += values[:, half:]


def finish(fast, me, x, cs, cotangent, margin, wos, w1_parts, w2, vec, bias):
    tokens, width = x.shape
    hidden = w2.shape[0] * w2.shape[1]
    rows = min(ROWS, tokens)
    natural = pl.BlockSpec((rows, width), lambda i, me: (i, 0))
    flipped = pl.BlockSpec((width, rows), lambda i, me: (0, i))
    once = pl.Buffered(1)
    outs = [
        shaped(bf16, tokens, width),
        shaped(bf16, 2, tokens, hidden // 2),
        shaped(bf16, 2, tokens, hidden // 2),
        shaped(bf16, 2, tokens, width),
        shaped(bf16, tokens, width),
        shaped(f32, tokens, width),
        shaped(bf16, width, tokens),
        shaped(f32, 8, width),
        shaped(f32, 8, hidden // 8),
    ]
    return prefetched(
        functools.partial(finish_kernel, fast, len(cs), len(wos)),
        me,
        (*cs, *wos, *w1_parts, x, w2, cotangent, margin, vec, bias),
        [pl.BlockSpec((c.shape[0], rows), lambda i, me: (0, i)) for c in cs]
        + [
            pl.BlockSpec((width, wo.shape[1]), lambda i, me: (3, 0), pipeline_mode=once)
            for wo in wos
        ]
        + [
            pl.BlockSpec(part.shape, lambda i, me: (0, 0, 0), pipeline_mode=once)
            for part in w1_parts
        ]
        + [
            natural,
            pl.BlockSpec(memory_space=pl.ANY),
            natural,
            pl.BlockSpec((1, rows), lambda i, me: (0, i)),
            full(8, width),
            full(8, hidden // 8),
        ],
        outs,
        out_specs=[
            natural,
            pl.BlockSpec((2, rows, hidden // 2), lambda i, me: (0, i, 0)),
            pl.BlockSpec((2, rows, hidden // 2), lambda i, me: (0, i, 0)),
            pl.BlockSpec((2, rows, width), lambda i, me: (0, i, 0)),
            natural,
            natural,
            flipped,
            full(8, width),
            full(8, hidden // 8),
        ],
        grid=(tokens // rows,),
        scratch=[
            pltpu.VMEM((rows, hidden), f32),
            pltpu.VMEM(w2.shape, bf16),
            pltpu.SemaphoreType.DMA((SLOTS,)),
        ],
        cost_estimate=cost(
            2 * tokens * width * (2 * width + 4 * hidden),
            tokens * width * 20 + tokens * hidden * 4 + hidden * width * 4,
            tokens * hidden * 2,
        ),
        name="finish",
    )


def finish_layout_kernel(*refs):
    (
        c_ref, x_ref, attn_ref, w1_ref, w2_ref, cot_ref, margin_ref, vec_ref, out_ref, da_ref, dz1_ref,
        dc_ref, small_ref, hidden_ref, one_ref, two_ref, du_ref, act_ref, low_ref, dy_ref, slope_ref,
    ) = refs
    pieces = FL // DL
    row = lambda number: vec_ref[number : number + 1, :]
    sums, hidden_sums = finish_rows(
        x_ref[...].T,
        c_ref[...],
        cot_ref[...].T,
        margin_ref[...],
        attn_ref[pl.ds(3 * DL, DL), :],
        lambda piece: w1_ref[pl.ds(piece * DL, DL), :],
        lambda piece: w2_ref[pl.ds(piece * DL, DL), :],
        lambda piece: row(8 + piece),
        row,
        pieces,
        (
            out_ref,
            [du_ref.at[:, pl.ds(piece * DL, DL)] for piece in range(pieces)],
            [act_ref.at[:, pl.ds(piece * DL, DL)] for piece in range(pieces)],
            low_ref, dy_ref, da_ref, dz1_ref, dc_ref, slope_ref,
        ),
        flipped=True,
    )
    small_ref[...] = jnp.zeros_like(small_ref)
    hidden_ref[...] = jnp.zeros_like(hidden_ref)
    for number, values in enumerate(sums):
        small_ref[number : number + 1, :] = values
    for piece, values in enumerate(hidden_sums):
        hidden_ref[piece : piece + 1, :] = values
    one_ref[...] = dot(du_ref[...], low_ref[...], 0, 0)
    two_ref[...] = dot(act_ref[...], dy_ref[...], 0, 0)


def finish_layout(x, c, cotangent, margin, attn, w1, w2, vec):
    width, tokens = x.shape
    hidden = w1.shape[0]
    return pl.pallas_call(
        finish_layout_kernel,
        out_shape=[
            shaped(bf16, width, tokens),
            shaped(bf16, tokens, width),
            shaped(f32, tokens, width),
            shaped(bf16, width, tokens),
            shaped(f32, 8, width),
            shaped(f32, 8, width),
            shaped(f32, hidden, width),
            shaped(f32, hidden, width),
        ],
        scratch_shapes=[
            pltpu.VMEM((tokens, hidden), bf16),
            pltpu.VMEM((tokens, hidden), bf16),
            pltpu.VMEM((tokens, width), bf16),
            pltpu.VMEM((tokens, width), bf16),
            pltpu.VMEM((tokens, hidden), f32),
        ],
        compiler_params=params(),
        cost_estimate=cost(2 * tokens * width * hidden * 10, tokens * width * 16),
        name="finish_layout",
    )(c, x, attn, w1, w2, cotangent, margin, vec)


def weight_grad_kernel(pairs, *refs):
    operands, (keep_ref, alpha_ref, beta_ref) = refs[: 2 * pairs], refs[2 * pairs :]
    total = None
    for pair in range(pairs):
        term = dot(operands[2 * pair][0], operands[2 * pair + 1][0], 0, 0)
        total = term if total is None else total + term
    total = total.reshape((2, 4) + keep_ref.shape[3:])
    keep_ref[0] = total[:, 0:2]
    for step, send_ref in enumerate((alpha_ref, beta_ref)):

        @pl.when(pl.program_id(0) == step)
        def _(send_ref=send_ref):
            send_ref[...] = total[:, 2:4].astype(bf16)


def weight_grad(which, *pairs):
    _, tokens, half = pairs[0][0].shape
    width = pairs[0][1].shape[2]
    height = 2 * half // SLOTS
    sent = shaped(bf16, 2, 2, height, width)
    return pl.pallas_call(
        functools.partial(weight_grad_kernel, len(pairs)),
        grid=(2,),
        in_specs=[
            pl.BlockSpec((1, tokens, half // 2), lambda i: (which, 0, i)),
            pl.BlockSpec((1, tokens, width), lambda i: (which, 0, 0)),
        ]
        * len(pairs),
        out_specs=[
            pl.BlockSpec((1, 2, 2, height, width), lambda i: (i, 0, 0, 0, 0)),
            whole(sent.shape),
            whole(sent.shape),
        ],
        out_shape=[shaped(f32, 2, 2, 2, height, width), sent, sent],
        compiler_params=params(),
        cost_estimate=cost(
            2 * tokens * half * width * len(pairs), 2 * tokens * (half + width) * len(pairs)
        ),
        name="weight_grad",
    )(*[operand for pair in pairs for operand in pair])


def input_grad_kernel(cuts, *refs):
    weight_refs, grad_refs = refs[: 3 * len(cuts)], refs[3 * len(cuts) : 3 * len(cuts) + 9]
    dz1_ref, dx_ref = refs[3 * len(cuts) + 9 :]
    wide = grad_refs[0].shape[0]
    total = None
    for number in range(3):
        for group in range(GROUPS):
            grad = grad_refs[number * GROUPS + group][...]
            start = group
            for piece, cut in enumerate(cuts):
                if 0 <= start < cut:
                    weight = weight_refs[number * len(cuts) + piece]
                    term = dot(weight[:, pl.ds(start * wide, wide)], grad, 1, 0)
                start -= cut
            total = term if total is None else total + term
    dx_ref[...] = total.T + dz1_ref[...]


def input_grad(attns, grads, dz1):
    tokens, width = dz1.shape
    rows = min(512, tokens)
    wide = grads[0].shape[0]
    cuts = [attn.shape[1] // wide for attn in attns]
    once = pl.Buffered(1)
    return pl.pallas_call(
        functools.partial(input_grad_kernel, cuts),
        grid=(tokens // rows,),
        in_specs=[
            pl.BlockSpec((width, attn.shape[1]), lambda i, number=number: (number, 0), pipeline_mode=once)
            for number in range(3)
            for attn in attns
        ]
        + [pl.BlockSpec((wide, rows), lambda i: (0, i))] * 9
        + [pl.BlockSpec((rows, width), lambda i: (i, 0))],
        out_specs=pl.BlockSpec((rows, width), lambda i: (i, 0)),
        out_shape=shaped(f32, tokens, width),
        compiler_params=params(),
        cost_estimate=cost(2 * tokens * width * width * 3, 14 * tokens * width),
        name="input_grad",
    )(*[attn for _ in range(3) for attn in attns], *grads, dz1)


def layout_end_kernel(fast, me_ref, *refs):
    x_ref, parts, c_ref = refs[0], [refs[1:4], refs[4:7], refs[7:10]], refs[10]
    bias_refs = refs[11:14]
    (
        da_ref, attn_ref, dz1_ref, one_ref, two_ref, small_ref, hidden_ref, small_l_ref,
        hidden_l_ref, keep_before_ref, send_before_ref, dx_ref, keep_ref, send_ref, rows_ref,
        sums_ref, units_ref,
    ) = refs[14:]
    me = place(fast, me_ref)
    tokens = x_ref.shape[1]
    height_l = 4 * DL // SLOTS
    blocks = SLOTS // 4
    xt = x_ref[...]
    total = None
    ones = jnp.ones((8, tokens), bf16)
    rows_ref[...] = jnp.zeros_like(rows_ref)
    for number, part_refs in enumerate(parts):
        grad = joined(part_refs, 0)
        rows_ref[pl.ds(number * blocks, blocks), 0:height_l, 0:DL] = dot(xt, grad, 1, 1).reshape(
            blocks, height_l, DL
        )
        term = dot(attn_ref[pl.ds(number * DL, DL), :], grad, 1, 0)
        total = term if total is None else total + term
        if number != 1:
            line = number // 2
            sums_ref[line : line + 1, :] = dot(ones, grad, 1, 1)[0:1]
    dx_ref[...] = total + dz1_ref[...].T
    rows_ref[pl.ds(3 * blocks, blocks), 0:height_l, 0:DL] = dot(
        c_ref[...], da_ref[...], 1, 0
    ).reshape(blocks, height_l, DL)
    rows_ref[:, height_l : 2 * height_l, 0:DL] = one_ref[...].reshape(SLOTS, height_l, DL)
    rows_ref[:, 2 * height_l : 3 * height_l, 0:DL] = two_ref[...].reshape(SLOTS, height_l, DL)
    sums_ref[2:8, :] = small_l_ref[0:6, :]
    sums_ref[8:12, :] = hidden_l_ref[0:4, :]
    bias = joined(bias_refs, 1)
    for slot in range(SLOTS):
        part, entry = slot // 4, slot % 4
        units_ref[owner(me, slot)] = hidden_ref[part : part + 1, entry * UNIT : (entry + 1) * UNIT]
    start = 3 * height_l
    for number in range(3 * SLOTS):
        line, column = number // 8, number % 8
        lanes = slice(column * UNIT, (column + 1) * UNIT)
        if line < 2:
            run = bias[line : line + 1, lanes]
        elif line < 8:
            run = small_ref[line - 2 : line - 1, lanes]
        else:
            run = units_ref[number - 64]
        at = start + number % 3
        rows_ref[number // 3, at : at + 1, 0:UNIT] = run
        rows_ref[number // 3, at : at + 1, UNIT : UNIT + UNIT_L] = sums_ref[
            line : line + 1, column * UNIT_L : (column + 1) * UNIT_L
        ]
    start = keep_before_ref.shape[2]
    at = pl.ds(start, rows_ref.shape[1])
    for slot in range(16):
        keep_ref[slot // 4, slot % 4, at, :] = rows_ref[owner(me, slot)]
        send_ref[slot // 4, slot % 4, at, :] = rows_ref[owner(me, slot + 16)].astype(bf16)
    keep_ref[:, :, 0:start, :] = keep_before_ref[...]
    send_ref[:, :, 0:start, :] = send_before_ref[...]


def layout_end(
    fast, me, x, parts, c, bias, da, attn, dz1, one, two, small, hidden, small_l, hidden_l, before
):
    width, tokens = x.shape
    height = 3 * 4 * DL // SLOTS + 8
    wide = GROUP * E
    operands = [x, *[part for three in parts for part in three], c, *bias, da, attn, dz1, one, two]
    operands += [small, hidden, small_l, hidden_l, *before]
    rows = before[0].shape[2] + height
    return prefetched(
        functools.partial(layout_end_kernel, fast),
        me,
        operands,
        [full(*operand.shape) for operand in operands],
        [
            shaped(f32, width, tokens),
            shaped(f32, 4, 4, rows, wide),
            shaped(bf16, 4, 4, rows, wide),
        ],
        scratch=[
            pltpu.VMEM((SLOTS, height, wide), f32),
            pltpu.VMEM((12, width), f32),
            pltpu.VMEM((SLOTS, 1, UNIT), f32),
        ],
        cost_estimate=cost(2 * tokens * width * width * 7, 24 * tokens * width),
        name="layout_end",
    )


def partners(mesh_sizes, plane, place):
    second = mesh_sizes[1]
    return [
        (a * second + b, (a ^ plane) * second + (b ^ place))
        for a in range(mesh_sizes[0])
        for b in range(mesh_sizes[1])
    ]


class Exchange:
    def __init__(self, sizes):
        self.sizes = sizes

    def __call__(self, value, plane=0, place=0):
        return lax.ppermute(value, AXES, partners(self.sizes, plane, place))


class Order:
    def __init__(self, depth=3):
        self.recent, self.depth = [], depth

    def wait(self, *values, seen=None):
        flat, tree = jax.tree.flatten(values)
        count = len(flat)
        done = lax.optimization_barrier(tuple(flat) + tuple(sum(self.recent, [])))
        kept = list(done[:count])
        if seen is not None:
            kept = kept[:seen] + sorted(kept[seen:], key=lambda leaf: leaf.size)[:1]
        else:
            kept = sorted(kept, key=lambda leaf: leaf.size)[:2]
        self.recent = (self.recent + [kept])[-self.depth :]
        return jax.tree.unflatten(tree, done[:count])


class Chain:
    def __init__(self, stages):
        self.stages = stages
        self.pending = next(stages)
        self.result = None


def step(sequence, *chains, values=()):
    pending = [chain.pending for chain in chains]
    pending, values = sequence.wait(pending, values, seen=len(jax.tree.leaves(pending)))
    for chain, arrived in zip(chains, pending):
        try:
            chain.pending = chain.stages.send(arrived)
        except StopIteration as stop:
            chain.pending, chain.result = None, stop.value
    return values


def gather_rows(exchange, own):
    z1, z2, z3 = yield (exchange(own, 0, 2), exchange(own, 0, 4), exchange(own, 0, 6))
    alpha, beta = jnp.stack([own, z1]), jnp.stack([z2, z3])
    over_x, over_y = yield (exchange(alpha, 1, 0), exchange(beta, 2, 0))
    alpha, beta = jnp.concatenate([alpha, over_x]), jnp.concatenate([beta, over_y])
    over_y, over_x = yield (exchange(alpha, 2, 0), exchange(beta, 1, 0))
    parts = [alpha, over_y, beta, over_x]
    other = yield tuple(exchange(part, 0, 1) for part in parts)
    return [*parts, *other]


def scatter_cores(exchange, keep, send):
    (received,) = yield (exchange(send, 0, 1),)
    both = keep + received.astype(f32)
    alpha, beta = both[0:2], both[2:4]
    return (
        yield from scatter_planes(
            exchange, alpha[:, 0:2], beta[:, 0:2], low(alpha[:, 2:4]), low(beta[:, 2:4])
        )
    )


def low(values):
    return values.astype(bf16)


def scatter_planes(exchange, alpha, beta, alpha_send, beta_send):
    over_x, over_y = yield (exchange(alpha_send, 1, 0), exchange(beta_send, 2, 0))
    return (
        yield from scatter_rest(exchange, alpha + over_x.astype(f32), beta + over_y.astype(f32))
    )


def scatter_rest(exchange, alpha, beta):
    over_y, over_x = yield (exchange(low(alpha[1]), 2, 0), exchange(low(beta[1]), 1, 0))
    alpha = alpha[0] + over_y.astype(f32)
    beta = beta[0] + over_x.astype(f32)
    first, second, third = yield (
        exchange(low(alpha[1]), 0, 2),
        exchange(low(beta[0]), 0, 4),
        exchange(low(beta[1]), 0, 6),
    )
    return (alpha[0] + first.astype(f32)) + (second.astype(f32) + third.astype(f32))


def on_device(sizes, *arguments):
    (
        text_input,
        layout_input,
        text_attn,
        text_ff_in,
        text_ff_out,
        text_vectors,
        layout_attn,
        layout_ff_in,
        layout_ff_out,
        layout_vectors,
        text_cotangent,
        layout_cotangent,
        margin,
        valid,
    ) = arguments
    devices = sizes[0] * sizes[1]
    fast = tuple(sizes) == (4, 8)
    tokens = text_input.shape[0]
    wide = GROUP * E
    rows_l = 4 * DL // SLOTS
    layout_flipped, layout_cotangent_flipped = layout_input.T, layout_cotangent.T
    valid_row, margin_row = valid.reshape(1, tokens), margin.reshape(1, tokens)
    gather_all = lambda own, axis=0: lax.all_gather(own, AXES, axis=axis, tiled=True)

    order = Order()
    if fast:
        me = (lax.axis_index("dp") * sizes[1] + lax.axis_index("fsdp")).astype(jnp.int32).reshape(1)
        exchange = Exchange(sizes)
        gather = lambda own: Chain(gather_rows(exchange, own))
        runs = [text_vectors.reshape(3, UNIT), layout_vectors.reshape(3, UNIT_L)]
        runs = jnp.pad(jnp.concatenate(runs, 1), ((0, 5), (0, D - UNIT - UNIT_L)))
        misc = jnp.stack([layout_attn, layout_ff_in.T, layout_ff_out], 1)
        misc = jnp.pad(misc, ((0, 0), (0, 0), (0, wide - DL))).reshape(rows_l, D)
        chain_a = gather(jnp.concatenate([text_attn, misc, runs], 0))
        own_b, own_c = step(order, chain_a, values=(text_ff_in.T, text_ff_out))
        chain_b = gather(own_b)
        (own_c,) = step(order, chain_a, values=(own_c,))
        w2 = gather_all(own_c)
        step(order, chain_a)
        step(order, chain_b)
        step(order, chain_a)
        begun = begin(me, chain_a.result, layout_flipped)
        begun = step(order, chain_b, values=begun)
        attn, attn_l, w1_l, w2_l, vec, hidden_bias, vec_l, layout_heads = begun
        attn = attn.reshape(4 * D, D)
        attn_l, w1_l, w2_l = [part.reshape(-1, DL) for part in (attn_l, w1_l, w2_l)]
    else:
        me = jnp.zeros((1,), jnp.int32)
        attn = gather_all(text_attn)
        w1, w2 = gather_all(text_ff_in, 1).T, gather_all(text_ff_out)
        attn_l, w1_l, w2_l = (
            gather_all(layout_attn), gather_all(layout_ff_in, 1).T, gather_all(layout_ff_out),
        )
        vec = gather_all(text_vectors).astype(f32).reshape(12, D)
        vec, hidden_bias = vec[0:8], vec[8:12].reshape(8, F // 8)
        vec_l = gather_all(layout_vectors).astype(f32).reshape(12, DL)
        layout_heads = layout_project(layout_flipped, attn_l, vec_l)
    heads = attend_forward(text_input, attn, vec, layout_heads, valid_row)
    if fast:
        (heads,) = step(order, chain_b, values=(heads,))
    q, k, v, probs, c, c_l = heads

    end_l = finish_layout(
        layout_flipped, c_l, layout_cotangent_flipped, margin_row, attn_l, w1_l, w2_l, vec_l
    )
    if fast:
        (end_l,) = step(order, chain_b, values=(end_l,))
        w1_parts = chain_b.result
    else:
        w1_parts = [w1[n * F // 8 : (n + 1) * F // 8].reshape(4, -1, D) for n in range(8)]
    w2 = w2.reshape(SLOTS, F // SLOTS, D)
    end = finish(
        fast, me, text_input, [c], text_cotangent, margin_row, [attn], w1_parts, w2, vec,
        hidden_bias,
    )
    out, wide_own, wide_other, thin, da, dz1, dc, small, hidden = end
    out_l, da_l, dz1_l, dc_l, small_l, hidden_l, grads_one_l, grads_two_l = end_l

    def backward(group, dc, before=()):
        return attend_backward(
            fast, me, q, k, v, group, layout_heads, probs, dc, dc_l, text_input, c, da, before
        )

    if fast:
        (wide_other, thin, dc) = order.wait(wide_other, thin, dc)
        coming = exchange(wide_other, 0, 1), exchange(thin, 0, 1)
        back_0 = backward(0, dc)
        (coming, back_0, dc) = order.wait(coming, back_0, dc)
        pairs = (wide_own, thin), coming
        first_plane = lambda grads: (exchange(grads[1], 1, 0), exchange(grads[2], 2, 0))
        grads_two = weight_grad(1, *pairs)
        (grads_two, pairs) = order.wait(grads_two, pairs)
        coming_two = first_plane(grads_two)
        grads_one = weight_grad(0, *pairs)
        (grads_one, dc) = order.wait(grads_one, dc)
        coming_one = first_plane(grads_one)
        back_1 = backward(1, dc, back_0[6:8])
        (coming_two, back_1, dc) = order.wait(coming_two, back_1, dc)
        chain_1 = Chain(scatter_cores(exchange, *back_1[6:8]))
        (coming_one,) = order.wait(coming_one)
        alpha, beta = [
            jnp.concatenate(
                [grads_one[0][n] + coming_one[n].astype(f32), grads_two[0][n] + coming_two[n].astype(f32)],
                2,
            )
            for n in range(2)
        ]
        chain_ff = Chain(scatter_rest(exchange, alpha, beta))
        (dc,) = step(order, chain_1, values=(dc,))
        back_2 = backward(2, dc)
        (back_2,) = order.wait(back_2)
    else:
        back_0 = backward(0, dc)
        back_1 = backward(1, dc, back_0[6:8])
        back_2 = backward(2, dc)
    backs = (back_0, back_1, back_2)
    dx_l, keep_m, send_m = layout_end(
        fast, me, layout_flipped, [[back[n] for back in backs] for n in (3, 4, 5)], c_l,
        [back[8] for back in backs], da_l, attn_l, dz1_l, grads_one_l, grads_two_l, small, hidden,
        small_l, hidden_l, back_2[6:8],
    )
    grads_x = [back[n] for n in range(3) for back in backs]
    rows_t = 4 * D // SLOTS

    if fast:
        (keep_m, send_m, dx_l, grads_x) = order.wait(keep_m, send_m, dx_l, grads_x)
        chain_2 = Chain(scatter_cores(exchange, keep_m, send_m))
        step(order, chain_ff)
        step(order, chain_1)
        (grads_x,) = step(order, chain_2, values=(grads_x,))
        dx = input_grad([attn], grads_x, dz1)
        (dx,) = step(order, chain_1, values=(dx,))
        step(order, chain_2)
        step(order, chain_ff)
        step(order, chain_2)
        step(order, chain_1)
        step(order, chain_2)
        g1, g2 = chain_ff.result[0 : F // SLOTS].T, chain_ff.result[F // SLOTS :]
        sums = (chain_1.result[0:rows_t], chain_1.result[rows_t:], chain_2.result[0:rows_t])
        ga = jnp.concatenate(sums, 1)
        gm = chain_2.result[rows_t:]
        tail = gm[3 * rows_l : 3 * rows_l + 3]
        small_grads = (
            tail[:, 0:UNIT].reshape(-1),
            gm[0:rows_l, 0:DL],
            gm[rows_l : 2 * rows_l, 0:DL].T,
            gm[2 * rows_l : 3 * rows_l, 0:DL],
            tail[:, UNIT : UNIT + UNIT_L].reshape(-1),
        )
    else:
        dx = input_grad([attn], grads_x, dz1)
        scatter = lambda values, axis=0: lax.psum_scatter(
            values, AXES, scatter_dimension=axis, tiled=True
        )
        blocks = lambda keep, send: jnp.concatenate([keep, send.astype(f32)]).reshape(
            (SLOTS,) + keep.shape[2:]
        )

        def slots(keep, alpha, beta):
            sent = jnp.stack([alpha, beta]).astype(f32)
            return jnp.concatenate([keep, sent], 2).reshape(-1, D)

        both = lambda which: jnp.concatenate(
            [slots(*weight_grad(which, (half, thin))) for half in (wide_own, wide_other)]
        )
        g1, g2 = scatter(both(0).T, 1), scatter(both(1))
        joint, last = blocks(*back_1[6:8]), blocks(keep_m, send_m)
        ga = [joint[:, 0:rows_t], joint[:, rows_t:], last[:, 0:rows_t]]
        ga = scatter(jnp.concatenate([part.reshape(4 * D, wide) for part in ga], 1))
        gm = last[:, rows_t:]
        part = lambda n: gm[:, n * rows_l : (n + 1) * rows_l, 0:DL].reshape(-1, DL)
        tail = gm[:, 3 * rows_l : 3 * rows_l + 3]
        small_grads = (
            scatter(tail[:, :, 0:UNIT].reshape(-1)),
            scatter(part(0)),
            scatter(part(1).T, 1),
            scatter(part(2)),
            scatter(tail[:, :, UNIT : UNIT + UNIT_L].reshape(-1)),
        )
    return (out, out_l.T, dx, dx_l.T, ga, g1, g2) + small_grads


def solution(mesh):
    rows, columns, flat = P(AXES, None), P(None, AXES), P(AXES)
    sizes = (mesh.shape["dp"], mesh.shape["fsdp"])
    return jax.shard_map(
        functools.partial(on_device, sizes),
        mesh=mesh,
        in_specs=(
            rows, rows, rows, columns, rows, flat, rows, columns, rows, flat, rows, rows, flat, flat,
        ),
        out_specs=(
            rows, rows, rows, rows, rows, columns, rows, flat, rows, columns, rows, flat,
        ),
        check_vma=False,
    )
```
